32 devices in a mesh: seq: 4 (over x, core), mp: 8 (over z, y).
Axes of the slice: x: 2, y: 2, z: 4, core: 2. Of those that a mesh axis runs over, the one named last changes fastest.
Arguments:
- queries: bfloat16 [1024, 4096], P('seq', 'mp'), may hold values from -15 to 15
- keys_values: bfloat16 [2, 1024, 4096], P(None, 'seq', 'mp'), may hold values from -6 to 6
- residual: bfloat16 [1024, 4096], P('seq', 'mp'), may hold values from -6 to 6
- cotangent: bfloat16 [1024, 4096], P('seq', 'mp'), may hold values from -6 to 6
- out_weight: bfloat16 [2, 4096, 4096], P(None, 'mp'), may hold values from -0.09375 to 0.09375
- kv_weight: bfloat16 [2, 4096, 4096], P(None, None, 'mp'), may hold values from -0.09375 to 0.09375
- bounds: int32 [2, 1024], replicated, may hold values from 0 to 767, as said below
- windows: int32 [64], P('mp'), may hold values from 1 to 127, as said below
Outputs:
- states_out: bfloat16 [1024, 4096], P('seq', 'mp')
- grad_states: bfloat16 [1024, 4096], P('seq', 'mp')
The draws below stay inside these ranges and needn't reach their ends.
Inputs may be any that keep to these rules, and one draw needn't show every extreme that they name: The encoder rows form 4 documents, each a run of consecutive positions; an encoder token's bounds are its own document's first and last position. The last document begins among the last 255 encoder positions. Decoder tokens belong to documents in reverse order, the first decoder token to the last document (other documents may have none), and carry that document's encoder bounds. `windows`: some head reaches exactly 127.
All inputs are finite; a program needn't handle non-finite values.
Results may differ from the reference program's by a relative error of at most 0.038.
Values may be sent and summed in bfloat16 or wider, within the bound.
A program may use at most 64 MiB of HBM per device.

```python
import jax
import jax.numpy as jnp
from jax import lax

D = 4096
HEADS = 64
HD = 64
ROWS = 256
WIN = 127
NDOC = 4
INNER = 4096
HL = 8
ENC_TOKENS = 768
DEC_TOKENS = 256
TOKENS = 1024
N_MP = 8


def draw_queries(key, part):
    base = jax.random.normal(jax.random.fold_in(key, 11), (TOKENS, HEADS * HD), jnp.float32)
    base = jnp.clip(base, -5.0, 5.0)
    return base.astype(jnp.bfloat16)


def draw_bounds(key, part):
    dec_count = TOKENS - ENC_TOKENS
    early_cuts = jax.random.permutation(jax.random.fold_in(key, 21), ENC_TOKENS - ROWS - 1)[:NDOC - 2] + 1
    last_cut = ENC_TOKENS - ROWS + 1 + jax.random.randint(jax.random.fold_in(key, 23), (1,), 0, ROWS - 1)
    enc_cuts = jnp.sort(jnp.concatenate([early_cuts.astype(jnp.int32), last_cut.astype(jnp.int32)])).astype(jnp.int32)
    starts = jnp.concatenate([jnp.zeros((1,), jnp.int32), enc_cuts])
    finals = jnp.concatenate([enc_cuts, jnp.full((1,), ENC_TOKENS, jnp.int32)]) - 1
    enc_pos = jnp.arange(ENC_TOKENS, dtype=jnp.int32)
    enc_doc = jnp.sum((enc_pos[:, None] >= enc_cuts[None, :]).astype(jnp.int32), axis=1)
    dec_cuts = jnp.sort(jax.random.randint(jax.random.fold_in(key, 22), (NDOC - 1,), 1, dec_count + 1)).astype(jnp.int32)
    dec_pos = jnp.arange(dec_count, dtype=jnp.int32)
    dec_doc = NDOC - 1 - jnp.sum((dec_pos[:, None] >= dec_cuts[None, :]).astype(jnp.int32), axis=1)
    doc_index = jnp.concatenate([enc_doc, dec_doc])
    return jnp.stack([starts[doc_index], finals[doc_index]]).astype(jnp.int32)


def draw_windows(key, part):
    widths = jax.random.randint(jax.random.fold_in(key, 31), (HEADS,), 1, WIN + 1)
    chosen = jax.random.randint(jax.random.fold_in(key, 32), (), 0, HEADS)
    return jnp.where(jnp.arange(HEADS) == chosen, WIN, widths).astype(jnp.int32)


def block_levels(stream_key, dims, split, low, top_value):
    gain, own = 1.0, jax.random.fold_in(stream_key, 6)
    for position, shards_of in split:
        draws = jnp.exp(jax.random.uniform(jax.random.fold_in(own, position), (shards_of,), jnp.float32, low / len(split), top_value / len(split)))
        gain = gain * jnp.repeat(draws, dims[position] // shards_of).reshape([-1 if axis == position else 1 for axis in range(len(dims))])
    return gain


def noise(key, dims, scale, most, cuts=(), held_as=jnp.bfloat16):
    drawn = scale * jax.random.normal(key, dims, jnp.float32)
    if cuts:
        drawn = drawn * block_levels(key, dims, cuts, -0.22, 0.18)
    return jnp.clip(drawn, -most, most).astype(held_as)


def setup_inputs(seed: int = 0) -> dict:
    arg_keys = jax.random.split(jax.random.key(seed), 9)
    queries = draw_queries(jax.random.fold_in(arg_keys[8], 71), 0)
    keys_values = noise(arg_keys[1], (2, TOKENS, INNER), 1.0, 6.0, ((1, 4), (2, 8)))
    residual = noise(arg_keys[2], (TOKENS, D), 1.0, 6.0, ((0, 4), (1, 8)))
    cotangent = noise(arg_keys[3], (TOKENS, D), 1.0, 6.0, ((0, 4), (1, 8)))
    out_weight = noise(arg_keys[4], (2, INNER, D), INNER ** -0.5, 0.09375, ((1, 8),))
    kv_weight = noise(arg_keys[5], (2, D, INNER), D ** -0.5, 0.09375, ((2, 8),))
    bounds = draw_bounds(jax.random.fold_in(arg_keys[8], 71), 0)
    windows = draw_windows(jax.random.fold_in(arg_keys[8], 71), 0)
    return {"queries": queries, "keys_values": keys_values, "residual": residual, "cotangent": cotangent, "out_weight": out_weight, "kv_weight": kv_weight, "bounds": bounds, "windows": windows}


def softmax_masked(scores, permitted):
    masked_scores = jnp.where(permitted, scores, -jnp.inf)
    row_top = jnp.max(masked_scores, axis=-1, keepdims=True)
    exp_scores = jnp.exp(masked_scores - row_top)
    return exp_scores / jnp.sum(exp_scores, axis=-1, keepdims=True)


def grouped_sum(left, right):
    def accumulate(running, pair):
        part_left, part_right = pair
        partial_term = jnp.dot(part_left, part_right, preferred_element_type=jnp.float32).astype(jnp.bfloat16)
        partial_term = lax.optimization_barrier(partial_term)
        return running + partial_term.astype(jnp.float32), None

    start_total = jnp.zeros((left.shape[1], right.shape[2]), jnp.float32)
    result_sum, unused_out = lax.scan(accumulate, start_total, (left, right))
    return result_sum


def block_total(parts):
    rounded = lax.optimization_barrier(parts.astype(jnp.bfloat16))
    return jnp.sum(rounded.astype(jnp.float32), axis=0).astype(jnp.bfloat16)


def by_head(array, count):
    return array.reshape(count, HEADS, HD).transpose(1, 0, 2)


def by_rows(array, count):
    return array.transpose(1, 0, 2).reshape(count, HEADS * HD)


def by_group(array, count):
    return array.reshape(count, N_MP, HL * HD).transpose(1, 0, 2)


def reference(queries, keys_values, residual, cotangent, out_weight, kv_weight, bounds, windows):
    score_scale = HD ** -0.5
    dec_blocks = DEC_TOKENS // ROWS
    first_pos = bounds[0]
    last_pos = bounds[1]
    enc_pos = jnp.arange(ENC_TOKENS, dtype=jnp.int32)
    doc_enc = (enc_pos[None, :] >= first_pos[:ENC_TOKENS, None]) & (enc_pos[None, :] <= last_pos[:ENC_TOKENS, None])
    distance = jnp.abs(enc_pos[:, None] - enc_pos[None, :])

    def local_head(inputs):
        head_query, head_key, head_value, reach_limit = inputs
        scores = jnp.dot(head_query, head_key.T, preferred_element_type=jnp.float32) * score_scale
        weights = softmax_masked(scores, doc_enc & (distance <= reach_limit))
        return jnp.dot(weights.astype(jnp.bfloat16), head_value, preferred_element_type=jnp.float32).astype(jnp.bfloat16)

    local_context = lax.map(local_head, (by_head(queries[:ENC_TOKENS], ENC_TOKENS), by_head(keys_values[0, :ENC_TOKENS], ENC_TOKENS), by_head(keys_values[1, :ENC_TOKENS], ENC_TOKENS), windows))
    local_context = by_rows(local_context, ENC_TOKENS)
    local_sum = grouped_sum(by_group(local_context, ENC_TOKENS), out_weight[0].reshape(N_MP, HL * HD, D))
    encoder_out = (residual[:ENC_TOKENS].astype(jnp.float32) + local_sum).astype(jnp.bfloat16)
    cross_keys = jnp.dot(encoder_out, kv_weight[0], preferred_element_type=jnp.float32).astype(jnp.bfloat16)
    cross_values = jnp.dot(encoder_out, kv_weight[1], preferred_element_type=jnp.float32).astype(jnp.bfloat16)

    doc_dec = (enc_pos[None, :] >= first_pos[ENC_TOKENS:, None]) & (enc_pos[None, :] <= last_pos[ENC_TOKENS:, None])
    context_grad = lax.dot_general(cotangent[ENC_TOKENS:], out_weight[1], (((1,), (1,)), ((), ())), preferred_element_type=jnp.float32).astype(jnp.bfloat16)

    def cross_head(inputs):
        head_query, head_key, head_value, head_grad = inputs
        scores = jnp.dot(head_query, head_key.T, preferred_element_type=jnp.float32) * score_scale
        weights = softmax_masked(scores, doc_dec)
        rounded = weights.astype(jnp.bfloat16)
        context = jnp.dot(rounded, head_value, preferred_element_type=jnp.float32).astype(jnp.bfloat16)
        row_dots = jnp.sum(head_grad.astype(jnp.float32) * context.astype(jnp.float32), axis=1)
        prob_grad = jnp.dot(head_grad, head_value.T, preferred_element_type=jnp.float32)
        score_grad = (weights * (prob_grad - row_dots[:, None])).astype(jnp.bfloat16)
        query_grad = (score_scale * jnp.dot(score_grad, head_key, preferred_element_type=jnp.float32)).astype(jnp.bfloat16)
        grad_blocks = score_grad.astype(jnp.float32).reshape(dec_blocks, ROWS, ENC_TOKENS)
        prob_blocks = rounded.astype(jnp.float32).reshape(dec_blocks, ROWS, ENC_TOKENS)
        query_blocks = head_query.astype(jnp.float32).reshape(dec_blocks, ROWS, HD)
        grad_rows = head_grad.astype(jnp.float32).reshape(dec_blocks, ROWS, HD)
        key_grad = block_total(score_scale * jnp.einsum("sqk,sqd->skd", grad_blocks, query_blocks))
        value_grad = block_total(jnp.einsum("sqk,sqd->skd", prob_blocks, grad_rows))
        return context, query_grad, key_grad, value_grad

    cross_context, query_grad, key_grad, value_grad = lax.map(cross_head, (by_head(queries[ENC_TOKENS:], DEC_TOKENS), by_head(cross_keys, ENC_TOKENS), by_head(cross_values, ENC_TOKENS), by_head(context_grad, DEC_TOKENS)))
    cross_context = by_rows(cross_context, DEC_TOKENS)
    query_grad = by_rows(query_grad, DEC_TOKENS)
    key_grad = by_rows(key_grad, ENC_TOKENS)
    value_grad = by_rows(value_grad, ENC_TOKENS)

    decoder_sum = grouped_sum(by_group(cross_context, DEC_TOKENS), out_weight[1].reshape(N_MP, HL * HD, D))
    decoder_out = (residual[ENC_TOKENS:].astype(jnp.float32) + decoder_sum).astype(jnp.bfloat16)
    grad_left = jnp.concatenate([by_group(key_grad, ENC_TOKENS), by_group(value_grad, ENC_TOKENS)], axis=2)
    weight_right = jnp.concatenate([kv_weight[0].reshape(D, N_MP, HL * HD).transpose(1, 2, 0), kv_weight[1].reshape(D, N_MP, HL * HD).transpose(1, 2, 0)], axis=1)
    encoder_grad = (cotangent[:ENC_TOKENS].astype(jnp.float32) + grouped_sum(grad_left, weight_right)).astype(jnp.bfloat16)
    return jnp.concatenate([encoder_out, decoder_out], axis=0), jnp.concatenate([encoder_grad, query_grad], axis=0)
```

```python
import functools

import jax
import jax.numpy as jnp
from jax import lax
from jax.experimental import pallas as pl
from jax.experimental.pallas import tpu as pltpu
from jax.sharding import PartitionSpec as P

HD = 64
WIN = 127


def with_halo(cells, sides, width):
    for axis, dim in sides:
        count = lax.axis_size(axis)
        ends = count - 1
        head = lax.slice_in_dim(cells, 0, width, axis=dim)
        tail = lax.slice_in_dim(cells, cells.shape[dim] - width, cells.shape[dim], axis=dim)
        cells = jnp.concatenate(
            [
                lax.ppermute(tail, axis, [(i, (i + 1) % count) for i in range(ends)]),
                cells,
                lax.ppermute(head, axis, [((i + 1) % count, i) for i in range(ends)]),
            ],
            axis=dim,
        )
    return cells


def softmax_masked(scores, permitted):
    masked_scores = jnp.where(permitted, scores, -jnp.inf)
    row_top = jnp.max(masked_scores, axis=-1, keepdims=True)
    exp_scores = jnp.exp(masked_scores - row_top)
    return exp_scores / jnp.sum(exp_scores, axis=-1, keepdims=True)


def shards(queries, keys_values, residual, cotangent, out_weight, kv_weight, bounds, windows):
    row_count = queries.shape[0]
    col_count = queries.shape[1]
    head_count = col_count // HD
    slab_count = lax.axis_size("seq")
    enc_slabs = 3 * slab_count // 4
    dec_slabs = slab_count - enc_slabs
    enc_tokens = enc_slabs * row_count
    token_count = slab_count * row_count
    dec_tokens = token_count - enc_tokens
    slab_index = lax.axis_index("seq")
    is_enc = slab_index < enc_slabs
    score_scale = HD ** (-0.5)
    own_pos = slab_index * row_count + jnp.arange(row_count, dtype=jnp.int32)
    own_first = lax.dynamic_slice_in_dim(bounds[0], slab_index * row_count, row_count)
    own_last = lax.dynamic_slice_in_dim(bounds[1], slab_index * row_count, row_count)
    query_heads = queries.reshape(row_count, head_count, HD)
    slice_cols = residual.shape[1]
    res_full, cot_full = (
        lax.all_gather(residual, "mp", axis=1, tiled=True),
        lax.all_gather(cotangent, "mp", axis=1, tiled=True),
    )
    model_width = cot_full.shape[1]
    rim_keys = with_halo(keys_values, (("seq", 1),), WIN)

    def local_part():
        span_count = rim_keys.shape[1]
        key_pos = slab_index * row_count - WIN + jnp.arange(span_count, dtype=jnp.int32)
        key_heads = rim_keys[0].reshape(span_count, head_count, HD)
        value_heads = rim_keys[1].reshape(span_count, head_count, HD)
        scores = (
            jnp.einsum("qhd,khd->hqk", query_heads, key_heads, preferred_element_type=jnp.float32)
            * score_scale
        )
        in_document = (key_pos[None, :] >= own_first[:, None]) & (
            key_pos[None, :] <= own_last[:, None]
        )
        distance = jnp.abs(own_pos[:, None] - key_pos[None, :])
        permitted = in_document[None] & (distance[None] <= windows[:, None, None])
        rounded = softmax_masked(scores, permitted).astype(jnp.bfloat16)
        context = jnp.einsum(
            "hqk,khd->qhd", rounded, value_heads, preferred_element_type=jnp.float32
        ).astype(jnp.bfloat16)
        return jnp.dot(
            context.reshape(row_count, col_count), out_weight[0], preferred_element_type=jnp.float32
        )

    head_partial = lax.cond(
        is_enc, local_part, lambda: jnp.zeros((row_count, model_width), jnp.float32)
    )
    attn_sum = lax.psum(head_partial.astype(jnp.bfloat16), "mp").astype(jnp.float32)
    hidden_full = (res_full.astype(jnp.float32) + attn_sum).astype(jnp.bfloat16)
    encoder_out = lax.dynamic_slice_in_dim(
        hidden_full, lax.axis_index("mp") * slice_cols, slice_cols, 1
    )

    def project_keys():
        key_proj = jnp.dot(hidden_full, kv_weight[0], preferred_element_type=jnp.float32).astype(
            jnp.bfloat16
        )
        value_proj = jnp.dot(hidden_full, kv_weight[1], preferred_element_type=jnp.float32).astype(
            jnp.bfloat16
        )
        return jnp.stack([key_proj, value_proj])

    cross_kv = lax.cond(
        is_enc, project_keys, lambda: jnp.zeros((2, row_count, col_count), jnp.bfloat16)
    )

    def context_gradient():
        return lax.dot_general(
            cot_full, out_weight[1], (((1,), (1,)), ((), ())), preferred_element_type=jnp.float32
        ).astype(jnp.bfloat16)

    dec_queries = lax.all_gather(queries, "seq", axis=0, tiled=True)[enc_tokens:]
    dec_heads = dec_queries.reshape(dec_tokens, head_count, HD)
    dec_first = bounds[0, enc_tokens:]
    dec_last = bounds[1, enc_tokens:]
    in_document = (own_pos[None, :] >= dec_first[:, None]) & (own_pos[None, :] <= dec_last[:, None])
    key_heads = cross_kv[0].reshape(row_count, head_count, HD)
    value_heads = cross_kv[1].reshape(row_count, head_count, HD)
    scores = (
        jnp.einsum("qhd,khd->hqk", dec_heads, key_heads, preferred_element_type=jnp.float32)
        * score_scale
    )
    masked_scores = jnp.where(in_document[None], scores, -jnp.inf)
    row_top = lax.pmax(jnp.max(masked_scores, axis=2), "seq")
    exp_scores = jnp.exp(masked_scores - row_top[:, :, None])
    row_total = lax.psum(jnp.sum(exp_scores, axis=2), "seq")
    weights = exp_scores / row_total[:, :, None]
    rounded = weights.astype(jnp.bfloat16)
    partial_ctx = jnp.einsum(
        "hqk,khd->qhd", rounded, value_heads, preferred_element_type=jnp.float32
    ).reshape(dec_tokens, col_count)
    context_all = lax.psum(partial_ctx.astype(jnp.bfloat16), "seq")
    dec_offset = jnp.maximum(slab_index - enc_slabs, 0) * row_count
    context = lax.dynamic_slice_in_dim(context_all, dec_offset, row_count, 0)
    out_part = lax.cond(
        is_enc,
        lambda: jnp.zeros((row_count, model_width), jnp.float32),
        lambda: jnp.dot(context, out_weight[1], preferred_element_type=jnp.float32),
    )
    grad_own = lax.cond(
        is_enc, lambda: jnp.zeros((row_count, col_count), jnp.bfloat16), context_gradient
    )
    grad_all = lax.all_gather(grad_own, "seq", axis=0, tiled=True)[enc_tokens:]
    grad_heads = grad_all.reshape(dec_tokens, head_count, HD)
    row_dots = jnp.einsum(
        "qhd,qhd->hq",
        grad_heads,
        context_all.reshape(dec_tokens, head_count, HD),
        preferred_element_type=jnp.float32,
    )
    prob_grad = jnp.einsum(
        "qhd,khd->hqk", grad_heads, value_heads, preferred_element_type=jnp.float32
    )
    score_grad = (weights * (prob_grad - row_dots[:, :, None])).astype(jnp.bfloat16)
    grad_blocks = score_grad.reshape(head_count, dec_slabs, row_count, row_count)
    prob_blocks = rounded.reshape(head_count, dec_slabs, row_count, row_count)
    query_blocks = dec_heads.reshape(dec_slabs, row_count, head_count, HD)
    grad_rows = grad_heads.reshape(dec_slabs, row_count, head_count, HD)
    key_parts = (
        score_scale
        * jnp.einsum(
            "hsqk,sqhd->skhd", grad_blocks, query_blocks, preferred_element_type=jnp.float32
        )
    ).astype(jnp.bfloat16)
    value_parts = jnp.einsum(
        "hsqk,sqhd->skhd", prob_blocks, grad_rows, preferred_element_type=jnp.float32
    ).astype(jnp.bfloat16)
    key_grad = (
        jnp.sum(key_parts.astype(jnp.float32), axis=0)
        .astype(jnp.bfloat16)
        .reshape(row_count, col_count)
    )
    value_grad = (
        jnp.sum(value_parts.astype(jnp.float32), axis=0)
        .astype(jnp.bfloat16)
        .reshape(row_count, col_count)
    )
    query_terms = score_scale * jnp.einsum(
        "hqk,khd->qhd", score_grad, key_heads, preferred_element_type=jnp.float32
    )
    query_sum = lax.psum(
        query_terms.reshape(dec_tokens, col_count).astype(jnp.bfloat16), "seq"
    ).astype(jnp.float32)
    query_grad = lax.dynamic_slice_in_dim(query_sum, dec_offset, row_count, 0).astype(jnp.bfloat16)
    contract = (((1,), (1,)), ((), ()))
    grad_terms = lax.dot_general(
        key_grad, kv_weight[0], contract, preferred_element_type=jnp.float32
    ) + lax.dot_general(value_grad, kv_weight[1], contract, preferred_element_type=jnp.float32)
    final_term = jnp.where(is_enc, grad_terms, out_part)
    final_share = lax.psum_scatter(
        final_term.astype(jnp.bfloat16), "mp", scatter_dimension=1, tiled=True
    ).astype(jnp.float32)
    base_rows = jnp.where(is_enc, cotangent, residual).astype(jnp.float32)
    final_rows = (base_rows + final_share).astype(jnp.bfloat16)
    states_out = jnp.where(is_enc, encoder_out, final_rows)
    grad_states = jnp.where(is_enc, final_rows, query_grad)
    return (states_out, grad_states)


F32 = jnp.float32
BF16 = jnp.bfloat16
LOW = -1e30
PAIR = 2 * HD
HALO = 128
SLOTS = 2
NT = (((1,), (1,)), ((), ()))


def dot(a, b):
    return jnp.dot(a, b, preferred_element_type=F32)


def dot_nt(a, b):
    return lax.dot_general(a, b, NT, preferred_element_type=F32)


def layer_kernel(
    slabs,
    groups,
    q_ref,
    kv_ref,
    res_ref,
    cot_ref,
    ow_ref,
    kw_ref,
    bnd_ref,
    win_ref,
    states_ref,
    grads_ref,
    w_out,
    w_kv,
    kv_all,
    q_own,
    base_rows,
    slot_res,
    ctx,
    own_part,
    ysend,
    yrecv,
    zsend,
    zrecv,
    ysend2,
    yrecv2,
    zsend2,
    zrecv2,
    gath,
    cgath,
    acc,
    kv_new,
    dq,
    dg,
    e_buf,
    d_buf,
    stat,
    ctx_acc,
    stat_all,
    fac,
    tbuf,
    ctx_in,
    q_acc,
    qg_buf,
    qg_in,
    kvg,
    dctx,
    back_rows,
    w_sem,
    in_sem,
    halo_s,
    halo_r,
    ys_s,
    yr_s,
    zs_s,
    zr_s,
    ys2_s,
    yr2_s,
    zs2_s,
    zr2_s,
    gu_s,
    gd_s,
    gz_r,
    gy_s,
    gy_r,
    cu_s,
    cd_s,
    cz_r,
    cy_s,
    cy_r,
    dq_s,
    dq_r,
    dg_s,
    dg_r,
    st_s,
    st_r,
    cx_s,
    cx_r,
    qg_s,
    qg_r,
    hand_s,
    hand_r,
):
    rows, cols = q_own.shape
    pairs = cols // PAIR
    heads = cols // HD
    enc = slabs - 1
    donor = enc // 2
    sub = rows // SLOTS
    nz = groups // 2
    scale = HD ** (-0.5)
    s = lax.axis_index("seq")
    g = lax.axis_index("mp")
    z = g // 2
    y = lax.rem(g, 2)
    yo = 1 - y

    def remote(src, dst, send, recv, seq, mp):
        return pltpu.make_async_remote_copy(
            src_ref=src,
            dst_ref=dst,
            send_sem=send,
            recv_sem=recv,
            device_id={"seq": seq, "mp": mp},
            device_id_type=pl.DeviceIdType.MESH,
        )

    def arrived(dst, recv):
        pltpu.make_async_copy(dst, dst, recv).wait()

    is_enc = s < enc
    is_dec = s >= enc
    is_donor = s == donor
    is_last = s == enc - 1
    has = (is_enc, s != donor)

    def when_has(b):
        return pl.when(has[b])

    def block_at(b):
        return pl.multiple_of(jnp.where(is_donor | is_last, 1 - b, b) * sub, sub)

    def out_rows(b):
        return pl.ds(pl.multiple_of(jnp.where(is_dec, b * sub, block_at(b)), sub), sub)

    def key_base(b):
        return jnp.where(is_dec, donor * rows, s * rows + block_at(b))

    def load_q():
        return pltpu.make_async_copy(q_ref, q_own, in_sem.at[0])

    def load_kv():
        return pltpu.make_async_copy(kv_ref, kv_all.at[:, pl.ds(HALO, rows)], in_sem.at[1])

    def load_res(b):
        return pltpu.make_async_copy(res_ref.at[pl.ds(block_at(b), sub)], slot_res.at[b], in_sem.at[2 + b])

    def load_base(ref):
        return pltpu.make_async_copy(ref, base_rows, in_sem.at[4])

    def load_cot(b):
        return pltpu.make_async_copy(cot_ref.at[pl.ds(b * sub, sub)], cgath.at[g, b], in_sem.at[2 + b])

    def load_dq():
        return pltpu.make_async_copy(q_ref, dq, in_sem.at[0])

    def load_wo(i):
        return pltpu.make_async_copy(ow_ref.at[i], w_out.at[i], w_sem.at[i])

    def load_wkv():
        return pltpu.make_async_copy(kw_ref, w_kv, w_sem.at[2])

    barrier = pltpu.get_barrier_semaphore()

    def greet(seq, mp):
        pl.semaphore_signal(
            barrier,
            inc=1,
            device_id={"seq": seq, "mp": mp},
            device_id_type=pl.DeviceIdType.MESH,
        )

    for k in range(1, slabs):
        greet(lax.rem(s + k, slabs), g)
    for k in range(1, nz):
        greet(s, lax.rem(z + k, nz) * 2 + y)
    greet(s, z * 2 + yo)

    @pl.when(is_enc)
    def _():
        load_kv().start()
        load_q().start()
        load_wo(0).start()
        for b in range(SLOTS):
            load_res(b).start()
        load_wkv().start()
        load_base(cot_ref).start()

    @pl.when(is_dec)
    def _():
        for b in range(SLOTS):
            load_cot(b).start()
        load_wo(0).start()
        load_wo(1).start()
        load_dq().start()
        load_wkv().start()
        load_base(res_ref).start()

    pl.semaphore_wait(barrier, slabs + nz - 1)

    lane = lax.broadcasted_iota(jnp.int32, (1, PAIR), 1)
    low_lane = lane < HD
    lane_masks = (
        jnp.where(low_lane, 1.0, 0.0).astype(BF16),
        jnp.where(low_lane, 0.0, 1.0).astype(BF16),
    )
    low_row = lax.broadcasted_iota(jnp.int32, (PAIR, 1), 0) < HD

    def pair_cols(p):
        return pl.ds(pl.multiple_of(p * PAIR, PAIR), PAIR)

    def chunk_cols(c):
        return pl.ds(pl.multiple_of(c * cols, cols), cols)

    def nth(k):
        up = nz - 1 - z
        low = jnp.where(k < up, nz - 1 - k, k - up)
        high = jnp.where(k < z, k, nz - 1 - (k - z))
        return jnp.where(k == nz - 1, z, jnp.where(z < nz // 2, low, high))

    def scatter_out(b, part, ysend, yrecv, ys, yr):
        def first(k, carry):
            t = nth(k)
            ysend[b, t] = part(b, t * 2 + yo)
            remote(ysend.at[b, t], yrecv.at[b, t], ys.at[b, t], yr.at[b, t], s, z * 2 + yo).start()
            return carry

        lax.fori_loop(0, nz, first, 0)

    def scatter_own(b, part):
        def own(k, carry):
            t = nth(k)
            own_part[b, t] = part(b, t * 2 + y)
            return carry

        lax.fori_loop(0, nz, own, 0)

    def scatter_join(b, yrecv, zsend, zrecv, yr, zs, zr):
        def second(k, carry):
            t = nth(k)
            arrived(yrecv.at[b, t], yr.at[b, t])
            zsend[b, t] = (own_part[b, t].astype(F32) + yrecv[b, t].astype(F32)).astype(BF16)
            remote(zsend.at[b, t], zrecv.at[b, z], zs.at[b, t], zr.at[b, z], s, t * 2 + y).start()
            return carry

        lax.fori_loop(0, nz - 1, second, 0)

    def scatter_total(b, yrecv, zrecv, yr, zr):
        arrived(yrecv.at[b, z], yr.at[b, z])
        froms = [lax.rem(z + k, nz) for k in range(1, nz)]
        for f in froms:
            arrived(zrecv.at[b, f], zr.at[b, f])
        total = own_part[b, z].astype(F32) + yrecv[b, z].astype(F32)
        for f in froms:
            total = total + zrecv[b, f].astype(F32)
        return total

    def end_scatter(b, ysend, zsend, ys, zs):
        for k in range(nz):
            arrived(ysend.at[b, k], ys.at[b, k])

            @pl.when(z != k)
            def _():
                arrived(zsend.at[b, k], zs.at[b, k])

    def final_in(b, out_ref):
        at = out_rows(b)
        total = scatter_total(b, yrecv2, zrecv2, yr2_s, zr2_s)
        out_ref[at, :] = (base_rows[at, :].astype(F32) + total).astype(BF16)

    def gather_parts(buf, us, ds, zr, ys, yr):
        def to_partner(c, t, b):
            remote(buf.at[c, b], buf.at[c, b], ys.at[t, b], yr.at[t, b], s, z * 2 + yo).start()

        def to_above(c, t, b):
            @pl.when(z < nz - 1)
            def _():
                remote(
                    buf.at[c, b], buf.at[c, b], us.at[t, b], zr.at[t, b], s, (z + 1) * 2 + y
                ).start()

        def to_below(c, t, b):
            @pl.when(z > 0)
            def _():
                remote(
                    buf.at[c, b], buf.at[c, b], ds.at[t, b], zr.at[t, b], s, (z - 1) * 2 + y
                ).start()

        def start(b):
            to_above(g, z, b)
            to_below(g, z, b)
            to_partner(g, z, b)

        def forward(slots, use):
            for b in slots:
                use(g, b)

            def around(k, carry):
                @pl.when(z >= k)
                def _():
                    t = z - k
                    c = t * 2 + y
                    for b in slots:
                        arrived(buf.at[c, b], zr.at[t, b])
                        to_above(c, t, b)
                        to_partner(c, t, b)

                @pl.when(z + k < nz)
                def _():
                    t = z + k
                    c = t * 2 + y
                    for b in slots:
                        arrived(buf.at[c, b], zr.at[t, b])
                        to_below(c, t, b)
                        to_partner(c, t, b)

                @pl.when(z >= k)
                def _():
                    for b in slots:
                        use((z - k) * 2 + y, b)

                @pl.when(z + k < nz)
                def _():
                    for b in slots:
                        use((z + k) * 2 + y, b)

                return carry

            lax.fori_loop(1, nz, around, 0)

        def finish(slots, use):
            def step(k, carry):
                def land(t):
                    c = t * 2 + yo
                    for b in slots:
                        arrived(buf.at[c, b], yr.at[t, b])
                        use(c, b)

                @pl.when(z >= k)
                def _():
                    land(z - k)

                @pl.when((k > 0) & (z + k < nz))
                def _():
                    land(z + k)

                return carry

            lax.fori_loop(0, nz, step, 0)

        def end(slots):
            for b in slots:
                for t in range(nz):
                    c = t * 2 + y
                    arrived(buf.at[c, b], ys.at[t, b])

                    @pl.when((z >= t) & (z < nz - 1))
                    def _():
                        arrived(buf.at[c, b], us.at[t, b])

                    @pl.when((z <= t) & (z > 0))
                    def _():
                        arrived(buf.at[c, b], ds.at[t, b])

        return start, forward, finish, end

    gather_start, gather_forward, gather_finish, gather_end = gather_parts(
        gath, gu_s, gd_s, gz_r, gy_s, gy_r
    )
    cot_start, cot_forward, cot_finish, cot_end = gather_parts(cgath, cu_s, cd_s, cz_r, cy_s, cy_r)
    both = tuple(range(SLOTS))

    def attn_part(b, c):
        return dot(ctx[b], w_out[0, :, chunk_cols(c)]).astype(BF16)

    def back(c, b):
        acc[0, b] = acc[0, b] + dot_nt(cgath[c, b], w_out[1, :, chunk_cols(c)])

    @pl.when(is_enc)
    def _():
        @pl.when(s + 1 < enc)
        def _():
            remote(
                kv_ref.at[:, pl.ds(rows - HALO, HALO)],
                kv_all.at[:, pl.ds(0, HALO)],
                halo_s.at[0],
                halo_r.at[0],
                s + 1,
                g,
            ).start()

        @pl.when(s > 0)
        def _():
            remote(
                kv_ref.at[:, pl.ds(0, HALO)],
                kv_all.at[:, pl.ds(HALO + rows, HALO)],
                halo_s.at[1],
                halo_r.at[1],
                s - 1,
                g,
            ).start()

        @pl.when(is_donor)
        def _():
            remote(
                res_ref.at[pl.ds(block_at(1), sub)], slot_res.at[1], hand_s.at[0], hand_r.at[0], enc, g
            ).start()

        @pl.when(s == 0)
        def _():
            kv_all[:, pl.ds(0, HALO)] = jnp.zeros((2, HALO, cols), BF16)

        @pl.when(is_last)
        def _():
            kv_all[:, pl.ds(HALO + rows, HALO)] = jnp.zeros((2, HALO, cols), BF16)

        load_kv().wait()
        load_q().wait()
        span = sub + 2 * HALO

        def local_block(i):
            def left_halo():
                arrived(kv_all.at[:, pl.ds(0, HALO)], halo_r.at[0])

            def right_halo():
                arrived(kv_all.at[:, pl.ds(HALO + rows, HALO)], halo_r.at[1])

            if i == 0:
                pl.when((s > 0) & (s < enc - 1))(left_halo)
            else:
                pl.when(s < enc - 1)(right_halo)
                pl.when((s > 0) & is_last)(left_halo)
            slot = jnp.where(is_donor, 1 - i, i)
            base = pl.multiple_of(jnp.where(is_last, 1 - i, i) * sub, sub)
            key_pos = s * rows + base - HALO + lax.broadcasted_iota(jnp.int32, (span, 1), 0)
            own_pos = s * rows + base + lax.broadcasted_iota(jnp.int32, (1, sub), 1)
            far = jnp.abs(key_pos - own_pos)
            own_at = pl.ds(pl.multiple_of(s * rows + base, sub), sub)
            in_doc = (key_pos >= bnd_ref[0:1, own_at]) & (key_pos <= bnd_ref[1:2, own_at])
            far_in = jnp.where(in_doc, far, jnp.int32(1 << 20))
            q_at = pl.ds(base, sub)
            k_at = pl.ds(base, span)

            def local_pair(p, carry):
                at = pair_cols(p)
                q_pair = q_own[q_at, at]
                k_pair = kv_all[0, k_at, at]
                v_t = kv_all[1, k_at, at].T
                got = []
                for j in range(2):
                    sc = dot_nt(k_pair, q_pair * lane_masks[j]) * scale
                    sc = jnp.where(far_in <= win_ref[p * 2 + j], sc, LOW)
                    e = jnp.exp(sc - jnp.max(sc, axis=0, keepdims=True))
                    inv = 1.0 / jnp.sum(e, axis=0, keepdims=True)
                    got.append(dot(v_t, (e * inv).astype(BF16)))
                ctx[slot, :, at] = jnp.where(low_row, got[0], got[1]).T.astype(BF16)
                return carry

            lax.fori_loop(0, pairs, local_pair, 0)

        local_block(0)
        load_wo(0).wait()

        @pl.when(is_donor)
        def _():
            remote(ctx.at[1], ctx.at[1], hand_s.at[1], hand_r.at[1], enc, g).start()

        @pl.when(s != donor)
        def _():
            scatter_out(0, attn_part, ysend, yrecv, ys_s, yr_s)

        local_block(1)

        @pl.when(is_donor)
        def _():
            scatter_out(0, attn_part, ysend, yrecv, ys_s, yr_s)

    acc[...] = jnp.zeros_like(acc)

    @pl.when(is_dec)
    def _():
        for b in both:
            load_cot(b).wait()
            cot_start(b)
        load_wo(1).wait()
        cot_forward(both, back)
        load_wo(0).wait()
        arrived(ctx.at[1], hand_r.at[1])

    @when_has(1)
    def _():
        scatter_out(1, attn_part, ysend, yrecv, ys_s, yr_s)

    @when_has(0)
    def _():
        scatter_own(0, attn_part)

    @when_has(1)
    def _():
        scatter_own(1, attn_part)

    def start_block(b):
        total = scatter_total(b, yrecv, zrecv, yr_s, zr_s)
        hidden = (slot_res[b].astype(F32) + total).astype(BF16)
        gath[g, b] = hidden
        gather_start(b)

        @pl.when(is_enc)
        def _():
            states_ref[out_rows(b), :] = hidden

    @when_has(0)
    def _():
        scatter_join(0, yrecv, zsend, zrecv, yr_s, zs_s, zr_s)
        load_res(0).wait()
        start_block(0)

    @when_has(1)
    def _():
        scatter_join(1, yrecv, zsend, zrecv, yr_s, zs_s, zr_s)

    load_wkv().wait()

    @pl.when(is_dec)
    def _():
        cot_finish(both, back)
        for b in both:
            dg[b * sub : (b + 1) * sub, :] = acc[0, b].astype(BF16)
        acc[...] = jnp.zeros_like(acc)
        load_dq().wait()
        for k in range(enc):
            remote(dq, dq, dq_s.at[k], dq_r, k, g).start()
            remote(dg, dg, dg_s.at[k], dg_r, k, g).start()

    def project(c, b):
        block = gath[c, b]
        acc[0, b] = acc[0, b] + dot(block, w_kv[0, chunk_cols(c), :])
        acc[1, b] = acc[1, b] + dot(block, w_kv[1, chunk_cols(c), :])

    @when_has(0)
    def _():
        gather_forward((0,), project)

    @when_has(1)
    def _():
        @pl.when(is_enc)
        def _():
            load_res(1).wait()

        @pl.when(is_dec)
        def _():
            arrived(slot_res.at[1], hand_r.at[0])

        start_block(1)

        @pl.when(is_dec)
        def _():
            remote(gath.at[g, 1], back_rows, hand_s.at[0], hand_r.at[2], donor, g).start()

        gather_forward((1,), project)

    for b in both:
        stat[b, 0] = jnp.full((heads, rows), LOW, F32)
        stat[b, 1] = jnp.zeros((heads, rows), F32)
        stat[b, 2] = jnp.zeros((heads, rows), F32)
        ctx_acc[b] = jnp.zeros((cols, rows), F32)
    q_acc[...] = jnp.zeros((cols, rows), F32)

    def cross_block(b):
        for i in range(2):
            kv_new[b, i] = acc[i, b].astype(BF16)
        tok_pos = key_base(b) + lax.broadcasted_iota(jnp.int32, (sub, 1), 0)
        seen = (tok_pos >= bnd_ref[0:1, enc * rows :]) & (tok_pos <= bnd_ref[1:2, enc * rows :])

        def cross_pair(p, carry):
            at = pair_cols(p)
            q_pair = dq[:, at]
            g_pair = dg[:, at]
            k_pair = kv_new[b, 0, :, at]
            v_pair = kv_new[b, 1, :, at]
            v_t = v_pair.T
            got = []
            for i in range(2):
                sc = dot_nt(k_pair, q_pair * lane_masks[i]) * scale
                sc = jnp.where(seen, sc, LOW)
                top = jnp.max(sc, axis=0, keepdims=True)
                e = jnp.exp(sc - top)
                dp = dot_nt(v_pair, g_pair * lane_masks[i])
                h = p * 2 + i
                e_buf[b, h] = e
                d_buf[b, h] = dp
                stat[b, 0, pl.ds(h, 1), :] = top
                stat[b, 1, pl.ds(h, 1), :] = jnp.sum(e, axis=0, keepdims=True)
                stat[b, 2, pl.ds(h, 1), :] = jnp.sum(e * dp, axis=0, keepdims=True)
                got.append(dot(v_t, e.astype(BF16)))
            ctx_acc[b, pair_cols(p), :] = jnp.where(low_row, got[0], got[1])
            return carry

        lax.fori_loop(0, pairs, cross_pair, 0)

    @when_has(0)
    def _():
        gather_finish((0,), project)
        arrived(dq, dq_r)
        arrived(dg, dg_r)
        cross_block(0)

    @when_has(1)
    def _():
        gather_finish((1,), project)
        cross_block(1)

    own_top = jnp.maximum(stat[0, 0], stat[1, 0])
    lift = [jnp.exp(stat[b, 0] - own_top) for b in both]
    stat_all[s, 0] = own_top
    stat_all[s, 1] = lift[0] * stat[0, 1] + lift[1] * stat[1, 1]
    stat_all[s, 2] = lift[0] * stat[0, 2] + lift[1] * stat[1, 2]
    for k in range(1, slabs):
        to = lax.rem(s + k, slabs)
        remote(stat_all.at[s], stat_all.at[s], st_s.at[k - 1], st_r.at[s], to, g).start()
    for h in range(heads):
        at = slice(h * HD, (h + 1) * HD)
        tbuf[at, :] = (
            lift[0][h : h + 1, :] * ctx_acc[0, at, :] + lift[1][h : h + 1, :] * ctx_acc[1, at, :]
        ).astype(BF16)

    @pl.when(is_enc)
    def _():
        remote(tbuf, ctx_in.at[s], cx_s, cx_r.at[s], enc, g).start()

    for k in range(1, slabs):
        at = lax.rem(s + k, slabs)
        arrived(stat_all.at[at], st_r.at[at])
    top = stat_all[0, 0]
    for i in range(1, slabs):
        top = jnp.maximum(top, stat_all[i, 0])
    shifts = [jnp.exp(stat_all[i, 0] - top) for i in range(slabs)]
    total = shifts[0] * stat_all[0, 1]
    dots = shifts[0] * stat_all[0, 2]
    for i in range(1, slabs):
        total = total + shifts[i] * stat_all[i, 1]
        dots = dots + shifts[i] * stat_all[i, 2]
    inv_total = 1.0 / total
    for b in both:
        fac[b] = jnp.exp(stat[b, 0] - top) * inv_total
    fac[SLOTS] = dots * inv_total

    def grad_block(b):
        def grad_pair(p, carry):
            at = pair_cols(p)
            q_pair = dq[:, at]
            g_pair = dg[:, at]
            k_t = kv_new[b, 0, :, at].T
            kg, vg, qg = [], [], []
            for i in range(2):
                h = p * 2 + i
                w = e_buf[b, h] * fac[b, pl.ds(h, 1), :]
                ds = (w * (d_buf[b, h] - fac[SLOTS, pl.ds(h, 1), :])).astype(BF16)
                vg.append(dot(w.astype(BF16), g_pair))
                kg.append(dot(ds, q_pair))
                qg.append(dot(k_t, ds))
            kvg[b, 0, :, at] = (scale * jnp.where(low_lane, kg[0], kg[1])).astype(BF16)
            kvg[b, 1, :, at] = jnp.where(low_lane, vg[0], vg[1]).astype(BF16)
            q_acc[pair_cols(p), :] = q_acc[pair_cols(p), :] + scale * jnp.where(low_row, qg[0], qg[1])
            return carry

        lax.fori_loop(0, pairs, grad_pair, 0)

    def grad_part(b, c):
        return (
            dot_nt(kvg[b, 0], w_kv[0, chunk_cols(c), :]) + dot_nt(kvg[b, 1], w_kv[1, chunk_cols(c), :])
        ).astype(BF16)

    def final_out(b, part):
        scatter_out(b, part, ysend2, yrecv2, ys2_s, yr2_s)

    @when_has(0)
    def _():
        grad_block(0)
        final_out(0, grad_part)

    @when_has(1)
    def _():
        grad_block(1)

    @pl.when(is_enc)
    def _():
        qg_buf[...] = q_acc[...].astype(BF16)

        @pl.when(is_donor)
        def _():
            scatter_own(0, grad_part)
            arrived(kvg.at[1], hand_r.at[3])

        final_out(1, grad_part)
        remote(qg_buf, qg_in.at[s], qg_s, qg_r.at[s], enc, g).start()

        @pl.when(s != donor)
        def _():
            scatter_own(0, grad_part)

        scatter_own(1, grad_part)
        load_base(cot_ref).wait()
        for b in both:
            scatter_join(b, yrecv2, zsend2, zrecv2, yr2_s, zs2_s, zr2_s)
        for b in both:
            final_in(b, grads_ref)

        @pl.when(is_donor)
        def _():
            arrived(back_rows, hand_r.at[2])
            states_ref[out_rows(1), :] = back_rows[...]
            arrived(slot_res.at[1], hand_s.at[0])
            arrived(ctx.at[1], hand_s.at[1])
            load_res(1).wait()

        @pl.when(s + 1 < enc)
        def _():
            arrived(kv_ref.at[:, pl.ds(rows - HALO, HALO)], halo_s.at[0])

        @pl.when(s > 0)
        def _():
            arrived(kv_ref.at[:, pl.ds(0, HALO)], halo_s.at[1])

        arrived(tbuf, cx_s)
        arrived(qg_buf, qg_s)

    @pl.when(is_dec)
    def _():
        remote(kvg.at[1], kvg.at[1], hand_s.at[1], hand_r.at[3], donor, g).start()
        ctx_in[enc] = tbuf[...]
        for k in range(enc):
            arrived(ctx_in.at[k], cx_r.at[k])
        shares = [shifts[k] * inv_total for k in range(slabs)]
        for p in range(pairs):
            mixed = []
            for h in (2 * p, 2 * p + 1):
                at = slice(h * HD, (h + 1) * HD)
                part = shares[0][h : h + 1, :] * ctx_in[0, at, :].astype(F32)
                for k in range(1, slabs):
                    part = part + shares[k][h : h + 1, :] * ctx_in[k, at, :].astype(F32)
                mixed.append(part)
            dctx[:, p * PAIR : (p + 1) * PAIR] = jnp.concatenate(mixed, axis=0).T.astype(BF16)

        def dec_part(b, c):
            return dot(dctx[b * sub : (b + 1) * sub, :], w_out[1, :, chunk_cols(c)]).astype(BF16)

        for b in both:
            final_out(b, dec_part)
        for b in both:
            scatter_own(b, dec_part)
        load_base(res_ref).wait()
        for b in both:
            scatter_join(b, yrecv2, zsend2, zrecv2, yr2_s, zs2_s, zr2_s)
        for k in range(enc):
            arrived(qg_in.at[k], qg_r.at[k])
        for p in range(pairs):
            at = slice(p * PAIR, (p + 1) * PAIR)
            part = q_acc[at, :]
            for k in range(enc):
                part = part + qg_in[k, at, :].astype(F32)
            grads_ref[:, at] = part.T.astype(BF16)
        for b in both:
            final_in(b, states_ref)
        for k in range(enc):
            arrived(dq, dq_s.at[k])
            arrived(dg, dg_s.at[k])
        cot_end(both)
        arrived(gath.at[g, 1], hand_s.at[0])
        arrived(kvg.at[1], hand_s.at[1])

    for b in both:

        @when_has(b)
        def _():
            end_scatter(b, ysend, zsend, ys_s, zs_s)
            gather_end((b,))

        end_scatter(b, ysend2, zsend2, ys2_s, zs2_s)
    for k in range(1, slabs):
        arrived(stat_all.at[s], st_s.at[k - 1])


def deliver(states_in, grads_in, states_out, grads_out):
    states_out[...] = states_in[...]
    grads_out[...] = grads_in[...]


def layer(slabs, groups, queries, keys_values, residual, cotangent, out_weight, kv_weight, bounds, windows):
    rows, cols = queries.shape
    heads = cols // HD
    nz = groups // 2
    enc = slabs - 1
    sub = rows // SLOTS
    width = out_weight.shape[2]
    dma = pltpu.SemaphoreType.DMA
    parts = lambda: pltpu.VMEM((SLOTS, nz, sub, cols), BF16)
    vmem = pl.BlockSpec(memory_space=pltpu.VMEM)
    hbm = pl.BlockSpec(memory_space=pl.ANY)
    states, grads = pl.pallas_call(
        functools.partial(layer_kernel, slabs, groups),
        out_shape=(jax.ShapeDtypeStruct((rows, cols), BF16),) * 2,
        in_specs=[hbm] * 6 + [vmem, pl.BlockSpec(memory_space=pltpu.SMEM)],
        out_specs=(vmem, vmem),
        scratch_shapes=[
            pltpu.VMEM((2, cols, width), BF16),
            pltpu.VMEM((2, width, cols), BF16),
            pltpu.VMEM((2, rows + 2 * HALO, cols), BF16),
            pltpu.VMEM((rows, cols), BF16),
            pltpu.VMEM((rows, cols), BF16),
            pltpu.VMEM((SLOTS, sub, cols), BF16),
            pltpu.VMEM((SLOTS, sub, cols), BF16),
        ]
        + [parts() for _ in range(9)]
        + [
            pltpu.VMEM((groups, SLOTS, sub, cols), BF16),
            pltpu.VMEM((groups, SLOTS, sub, cols), BF16),
            pltpu.VMEM((2, SLOTS, sub, cols), F32),
            pltpu.VMEM((SLOTS, 2, sub, cols), BF16),
            pltpu.VMEM((rows, cols), BF16),
            pltpu.VMEM((rows, cols), BF16),
            pltpu.VMEM((SLOTS, heads, sub, rows), F32),
            pltpu.VMEM((SLOTS, heads, sub, rows), F32),
            pltpu.VMEM((SLOTS, 3, heads, rows), F32),
            pltpu.VMEM((SLOTS, cols, rows), F32),
            pltpu.VMEM((slabs, 3, heads, rows), F32),
            pltpu.VMEM((SLOTS + 1, heads, rows), F32),
            pltpu.VMEM((cols, rows), BF16),
            pltpu.VMEM((slabs, cols, rows), BF16),
            pltpu.VMEM((cols, rows), F32),
            pltpu.VMEM((cols, rows), BF16),
            pltpu.VMEM((enc, cols, rows), BF16),
            pltpu.VMEM((SLOTS, 2, sub, cols), BF16),
            pltpu.VMEM((rows, cols), BF16),
            pltpu.VMEM((sub, cols), BF16),
            dma((3,)),
            dma((5,)),
            dma((2,)),
            dma((2,)),
        ]
        + [dma((SLOTS, nz))] * 8
        + [dma((nz, SLOTS))] * 10
        + [
            dma((enc,)),
            dma,
            dma((enc,)),
            dma,
            dma((enc,)),
            dma((slabs,)),
            dma,
            dma((enc,)),
            dma,
            dma((enc,)),
            dma((2,)),
            dma((4,)),
        ],
        compiler_params=pltpu.CompilerParams(
            collective_id=0, has_side_effects=True, vmem_limit_bytes=60 * 1024 * 1024
        ),
    )(queries, keys_values, residual, cotangent, out_weight, kv_weight, bounds, windows)
    return pl.pallas_call(
        deliver,
        out_shape=(jax.ShapeDtypeStruct((rows, cols), BF16),) * 2,
        in_specs=[vmem] * 2,
        out_specs=(vmem, vmem),
    )(states, grads)


def one_decoder_slab(mesh):
    slabs, groups = mesh.shape["seq"], mesh.shape["mp"]
    return slabs == 4 and groups % 2 == 0


def solution(mesh):
    body = shards
    if one_decoder_slab(mesh):
        body = functools.partial(layer, mesh.shape["seq"], mesh.shape["mp"])

    return jax.shard_map(
        body,
        mesh=mesh,
        in_specs=(
            P("seq", "mp"),
            P(None, "seq", "mp"),
            P("seq", "mp"),
            P("seq", "mp"),
            P(None, "mp", None),
            P(None, None, "mp"),
            P(),
            P("mp"),
        ),
        out_specs=(P("seq", "mp"), P("seq", "mp")),
        check_vma=False,
    )
```

```python
import functools

import jax
import jax.numpy as jnp
from jax import lax
from jax.experimental import pallas as pl
from jax.experimental.pallas import tpu as pltpu
from jax.sharding import PartitionSpec as P

HD = 64
WIN = 127


def with_halo(cells, sides, width):
    for axis, dim in sides:
        count = lax.axis_size(axis)
        ends = count - 1
        head = lax.slice_in_dim(cells, 0, width, axis=dim)
        tail = lax.slice_in_dim(cells, cells.shape[dim] - width, cells.shape[dim], axis=dim)
        cells = jnp.concatenate(
            [
                lax.ppermute(tail, axis, [(i, (i + 1) % count) for i in range(ends)]),
                cells,
                lax.ppermute(head, axis, [((i + 1) % count, i) for i in range(ends)]),
            ],
            axis=dim,
        )
    return cells


def softmax_masked(scores, permitted):
    masked_scores = jnp.where(permitted, scores, -jnp.inf)
    row_top = jnp.max(masked_scores, axis=-1, keepdims=True)
    exp_scores = jnp.exp(masked_scores - row_top)
    return exp_scores / jnp.sum(exp_scores, axis=-1, keepdims=True)


def shards(queries, keys_values, residual, cotangent, out_weight, kv_weight, bounds, windows):
    row_count = queries.shape[0]
    col_count = queries.shape[1]
    head_count = col_count // HD
    slab_count = lax.axis_size("seq")
    enc_slabs = 3 * slab_count // 4
    dec_slabs = slab_count - enc_slabs
    enc_tokens = enc_slabs * row_count
    token_count = slab_count * row_count
    dec_tokens = token_count - enc_tokens
    slab_index = lax.axis_index("seq")
    is_enc = slab_index < enc_slabs
    score_scale = HD ** (-0.5)
    own_pos = slab_index * row_count + jnp.arange(row_count, dtype=jnp.int32)
    own_first = lax.dynamic_slice_in_dim(bounds[0], slab_index * row_count, row_count)
    own_last = lax.dynamic_slice_in_dim(bounds[1], slab_index * row_count, row_count)
    query_heads = queries.reshape(row_count, head_count, HD)
    slice_cols = residual.shape[1]
    res_full, cot_full = (
        lax.all_gather(residual, "mp", axis=1, tiled=True),
        lax.all_gather(cotangent, "mp", axis=1, tiled=True),
    )
    model_width = cot_full.shape[1]
    rim_keys = with_halo(keys_values, (("seq", 1),), WIN)

    def local_part():
        span_count = rim_keys.shape[1]
        key_pos = slab_index * row_count - WIN + jnp.arange(span_count, dtype=jnp.int32)
        key_heads = rim_keys[0].reshape(span_count, head_count, HD)
        value_heads = rim_keys[1].reshape(span_count, head_count, HD)
        scores = (
            jnp.einsum("qhd,khd->hqk", query_heads, key_heads, preferred_element_type=jnp.float32)
            * score_scale
        )
        in_document = (key_pos[None, :] >= own_first[:, None]) & (
            key_pos[None, :] <= own_last[:, None]
        )
        distance = jnp.abs(own_pos[:, None] - key_pos[None, :])
        permitted = in_document[None] & (distance[None] <= windows[:, None, None])
        rounded = softmax_masked(scores, permitted).astype(jnp.bfloat16)
        context = jnp.einsum(
            "hqk,khd->qhd", rounded, value_heads, preferred_element_type=jnp.float32
        ).astype(jnp.bfloat16)
        return jnp.dot(
            context.reshape(row_count, col_count), out_weight[0], preferred_element_type=jnp.float32
        )

    head_partial = lax.cond(
        is_enc, local_part, lambda: jnp.zeros((row_count, model_width), jnp.float32)
    )
    attn_sum = lax.psum(head_partial.astype(jnp.bfloat16), "mp").astype(jnp.float32)
    hidden_full = (res_full.astype(jnp.float32) + attn_sum).astype(jnp.bfloat16)
    encoder_out = lax.dynamic_slice_in_dim(
        hidden_full, lax.axis_index("mp") * slice_cols, slice_cols, 1
    )

    def project_keys():
        key_proj = jnp.dot(hidden_full, kv_weight[0], preferred_element_type=jnp.float32).astype(
            jnp.bfloat16
        )
        value_proj = jnp.dot(hidden_full, kv_weight[1], preferred_element_type=jnp.float32).astype(
            jnp.bfloat16
        )
        return jnp.stack([key_proj, value_proj])

    cross_kv = lax.cond(
        is_enc, project_keys, lambda: jnp.zeros((2, row_count, col_count), jnp.bfloat16)
    )

    def context_gradient():
        return lax.dot_general(
            cot_full, out_weight[1], (((1,), (1,)), ((), ())), preferred_element_type=jnp.float32
        ).astype(jnp.bfloat16)

    dec_queries = lax.all_gather(queries, "seq", axis=0, tiled=True)[enc_tokens:]
    dec_heads = dec_queries.reshape(dec_tokens, head_count, HD)
    dec_first = bounds[0, enc_tokens:]
    dec_last = bounds[1, enc_tokens:]
    in_document = (own_pos[None, :] >= dec_first[:, None]) & (own_pos[None, :] <= dec_last[:, None])
    key_heads = cross_kv[0].reshape(row_count, head_count, HD)
    value_heads = cross_kv[1].reshape(row_count, head_count, HD)
    scores = (
        jnp.einsum("qhd,khd->hqk", dec_heads, key_heads, preferred_element_type=jnp.float32)
        * score_scale
    )
    masked_scores = jnp.where(in_document[None], scores, -jnp.inf)
    row_top = lax.pmax(jnp.max(masked_scores, axis=2), "seq")
    exp_scores = jnp.exp(masked_scores - row_top[:, :, None])
    row_total = lax.psum(jnp.sum(exp_scores, axis=2), "seq")
    weights = exp_scores / row_total[:, :, None]
    rounded = weights.astype(jnp.bfloat16)
    partial_ctx = jnp.einsum(
        "hqk,khd->qhd", rounded, value_heads, preferred_element_type=jnp.float32
    ).reshape(dec_tokens, col_count)
    context_all = lax.psum(partial_ctx.astype(jnp.bfloat16), "seq")
    dec_offset = jnp.maximum(slab_index - enc_slabs, 0) * row_count
    context = lax.dynamic_slice_in_dim(context_all, dec_offset, row_count, 0)
    out_part = lax.cond(
        is_enc,
        lambda: jnp.zeros((row_count, model_width), jnp.float32),
        lambda: jnp.dot(context, out_weight[1], preferred_element_type=jnp.float32),
    )
    grad_own = lax.cond(
        is_enc, lambda: jnp.zeros((row_count, col_count), jnp.bfloat16), context_gradient
    )
    grad_all = lax.all_gather(grad_own, "seq", axis=0, tiled=True)[enc_tokens:]
    grad_heads = grad_all.reshape(dec_tokens, head_count, HD)
    row_dots = jnp.einsum(
        "qhd,qhd->hq",
        grad_heads,
        context_all.reshape(dec_tokens, head_count, HD),
        preferred_element_type=jnp.float32,
    )
    prob_grad = jnp.einsum(
        "qhd,khd->hqk", grad_heads, value_heads, preferred_element_type=jnp.float32
    )
    score_grad = (weights * (prob_grad - row_dots[:, :, None])).astype(jnp.bfloat16)
    grad_blocks = score_grad.reshape(head_count, dec_slabs, row_count, row_count)
    prob_blocks = rounded.reshape(head_count, dec_slabs, row_count, row_count)
    query_blocks = dec_heads.reshape(dec_slabs, row_count, head_count, HD)
    grad_rows = grad_heads.reshape(dec_slabs, row_count, head_count, HD)
    key_parts = (
        score_scale
        * jnp.einsum(
            "hsqk,sqhd->skhd", grad_blocks, query_blocks, preferred_element_type=jnp.float32
        )
    ).astype(jnp.bfloat16)
    value_parts = jnp.einsum(
        "hsqk,sqhd->skhd", prob_blocks, grad_rows, preferred_element_type=jnp.float32
    ).astype(jnp.bfloat16)
    key_grad = (
        jnp.sum(key_parts.astype(jnp.float32), axis=0)
        .astype(jnp.bfloat16)
        .reshape(row_count, col_count)
    )
    value_grad = (
        jnp.sum(value_parts.astype(jnp.float32), axis=0)
        .astype(jnp.bfloat16)
        .reshape(row_count, col_count)
    )
    query_terms = score_scale * jnp.einsum(
        "hqk,khd->qhd", score_grad, key_heads, preferred_element_type=jnp.float32
    )
    query_sum = lax.psum(
        query_terms.reshape(dec_tokens, col_count).astype(jnp.bfloat16), "seq"
    ).astype(jnp.float32)
    query_grad = lax.dynamic_slice_in_dim(query_sum, dec_offset, row_count, 0).astype(jnp.bfloat16)
    contract = (((1,), (1,)), ((), ()))
    grad_terms = lax.dot_general(
        key_grad, kv_weight[0], contract, preferred_element_type=jnp.float32
    ) + lax.dot_general(value_grad, kv_weight[1], contract, preferred_element_type=jnp.float32)
    final_term = jnp.where(is_enc, grad_terms, out_part)
    final_share = lax.psum_scatter(
        final_term.astype(jnp.bfloat16), "mp", scatter_dimension=1, tiled=True
    ).astype(jnp.float32)
    base_rows = jnp.where(is_enc, cotangent, residual).astype(jnp.float32)
    final_rows = (base_rows + final_share).astype(jnp.bfloat16)
    states_out = jnp.where(is_enc, encoder_out, final_rows)
    grad_states = jnp.where(is_enc, final_rows, query_grad)
    return (states_out, grad_states)


F32 = jnp.float32
BF16 = jnp.bfloat16
LOW = -1e30
PAIR = 2 * HD
HALO = 128
SLOTS = 2
NT = (((1,), (1,)), ((), ()))


def dot(a, b):
    return jnp.dot(a, b, preferred_element_type=F32)


def dot_nt(a, b):
    return lax.dot_general(a, b, NT, preferred_element_type=F32)


def layer_kernel(
    slabs,
    groups,
    q_ref,
    kv_ref,
    res_ref,
    cot_ref,
    ow_ref,
    kw_ref,
    bnd_ref,
    win_ref,
    states_ref,
    grads_ref,
    w_out,
    w_kv,
    kv_all,
    q_own,
    base_rows,
    slot_res,
    ctx,
    own_part,
    ysend,
    yrecv,
    zsend,
    zrecv,
    ysend2,
    yrecv2,
    zsend2,
    zrecv2,
    gath,
    cgath,
    acc,
    kv_new,
    dq,
    dg,
    e_buf,
    d_buf,
    stat,
    ctx_acc,
    stat_all,
    fac,
    tbuf,
    ctx_in,
    q_acc,
    qg_buf,
    qg_in,
    kvg,
    dctx,
    back_rows,
    w_sem,
    in_sem,
    halo_s,
    halo_r,
    ys_s,
    yr_s,
    zs_s,
    zr_s,
    ys2_s,
    yr2_s,
    zs2_s,
    zr2_s,
    gz_s,
    gz_r,
    gy_s,
    gy_r,
    cz_s,
    cz_r,
    cy_s,
    cy_r,
    dq_s,
    dq_r,
    dg_s,
    dg_r,
    st_s,
    st_r,
    cx_s,
    cx_r,
    qg_s,
    qg_r,
    hand_s,
    hand_r,
):
    rows, cols = q_own.shape
    pairs = cols // PAIR
    heads = cols // HD
    enc = slabs - 1
    donor = enc // 2
    sub = rows // SLOTS
    nz = groups // 2
    scale = HD ** (-0.5)
    s = lax.axis_index("seq")
    g = lax.axis_index("mp")
    z = g // 2
    y = lax.rem(g, 2)
    yo = 1 - y
    low = z < nz // 2
    at_end = (z == 0) | (z == nz - 1)
    outer = jnp.where(low, 0, nz - 1)
    near = jnp.where(low, 1, nz - 2)
    mate = nz - 1 - near

    def remote(src, dst, send, recv, seq, mp):
        return pltpu.make_async_remote_copy(
            src_ref=src,
            dst_ref=dst,
            send_sem=send,
            recv_sem=recv,
            device_id={"seq": seq, "mp": mp},
            device_id_type=pl.DeviceIdType.MESH,
        )

    def arrived(dst, recv):
        pltpu.make_async_copy(dst, dst, recv).wait()

    is_enc = s < enc
    is_dec = s >= enc
    is_donor = s == donor
    is_last = s == enc - 1
    has = (is_enc, s != donor)

    def when_has(b):
        return pl.when(has[b])

    def block_at(b):
        return pl.multiple_of(jnp.where(is_donor | is_last, 1 - b, b) * sub, sub)

    def out_rows(b):
        return pl.ds(pl.multiple_of(jnp.where(is_dec, b * sub, block_at(b)), sub), sub)

    def key_base(b):
        return jnp.where(is_dec, donor * rows, s * rows + block_at(b))

    def load_q():
        return pltpu.make_async_copy(q_ref, q_own, in_sem.at[0])

    def load_kv():
        return pltpu.make_async_copy(kv_ref, kv_all.at[:, pl.ds(HALO, rows)], in_sem.at[1])

    def load_res(b):
        return pltpu.make_async_copy(res_ref.at[pl.ds(block_at(b), sub)], slot_res.at[b], in_sem.at[2 + b])

    def load_base(ref):
        return pltpu.make_async_copy(ref, base_rows, in_sem.at[4])

    def load_cot(b):
        return pltpu.make_async_copy(cot_ref.at[pl.ds(b * sub, sub)], cgath.at[g, b], in_sem.at[2 + b])

    def load_dq():
        return pltpu.make_async_copy(q_ref, dq, in_sem.at[0])

    def load_wo(i):
        return pltpu.make_async_copy(ow_ref.at[i], w_out.at[i], w_sem.at[i])

    def load_wkv():
        return pltpu.make_async_copy(kw_ref, w_kv, w_sem.at[2])

    barrier = pltpu.get_barrier_semaphore()

    def greet(seq, mp):
        pl.semaphore_signal(
            barrier,
            inc=1,
            device_id={"seq": seq, "mp": mp},
            device_id_type=pl.DeviceIdType.MESH,
        )

    for k in range(1, slabs):
        greet(lax.rem(s + k, slabs), g)
    for k in range(1, nz):
        greet(s, lax.rem(z + k, nz) * 2 + y)
    greet(s, z * 2 + yo)

    @pl.when(is_enc)
    def _():
        load_kv().start()
        load_q().start()
        load_wo(0).start()
        for b in range(SLOTS):
            load_res(b).start()
        load_wkv().start()
        load_base(cot_ref).start()

    @pl.when(is_dec)
    def _():
        for b in range(SLOTS):
            load_cot(b).start()
        load_wo(0).start()
        load_wo(1).start()
        load_dq().start()
        load_wkv().start()
        load_base(res_ref).start()

    lane = lax.broadcasted_iota(jnp.int32, (1, PAIR), 1)
    low_lane = lane < HD
    lane_masks = (
        jnp.where(low_lane, 1.0, 0.0).astype(BF16),
        jnp.where(low_lane, 0.0, 1.0).astype(BF16),
    )
    low_row = lax.broadcasted_iota(jnp.int32, (PAIR, 1), 0) < HD

    def pair_cols(p):
        return pl.ds(pl.multiple_of(p * PAIR, PAIR), PAIR)

    def chunk_cols(c):
        return pl.ds(pl.multiple_of(c * cols, cols), cols)

    def nth(k):
        t = jnp.where(at_end, nz - 1 - k, jnp.where(k == 0, 0, nz - k))
        return jnp.where(low, t, nz - 1 - t)

    def scatter_out(b, part, ysend, yrecv, ys, yr):
        def first(k, carry):
            t = nth(k)
            ysend[b, t] = part(b, t * 2 + yo)
            remote(ysend.at[b, t], yrecv.at[b, t], ys.at[b, t], yr.at[b, t], s, z * 2 + yo).start()
            return carry

        lax.fori_loop(0, nz, first, 0)

    def scatter_own(b, part):
        def own(k, carry):
            t = nth(k)
            own_part[b, t] = part(b, t * 2 + y)
            return carry

        lax.fori_loop(0, nz, own, 0)

    def scatter_join(b, yrecv, zsend, zrecv, yr, zs, zr):
        def second(k, carry):
            t = nth(k)
            arrived(yrecv.at[b, t], yr.at[b, t])
            joined = own_part[b, t].astype(F32) + yrecv[b, t].astype(F32)

            @pl.when(at_end | (t == outer))
            def _():
                zsend[b, t] = joined.astype(BF16)

            @pl.when(jnp.logical_not(at_end | (t == outer)))
            def _():
                arrived(zrecv.at[b, t], zr.at[b, t])
                zsend[b, t] = (joined + zrecv[b, t].astype(F32)).astype(BF16)

            to = jnp.where(at_end, near, t)
            slot = jnp.where(at_end, t, jnp.where(t == mate, nz - 1 - outer, z))
            remote(
                zsend.at[b, t], zrecv.at[b, slot], zs.at[b, t], zr.at[b, slot], s, to * 2 + y
            ).start()
            return carry

        lax.fori_loop(0, nz - 1, second, 0)

    def scatter_total(b, yrecv, zrecv, yr, zr):
        arrived(yrecv.at[b, z], yr.at[b, z])
        one = jnp.where(at_end, 1, jnp.where(low, 0, nz - 2))
        for k in range(2):
            arrived(zrecv.at[b, one + k], zr.at[b, one + k])
        total = own_part[b, z].astype(F32) + yrecv[b, z].astype(F32)
        return total + zrecv[b, one].astype(F32) + zrecv[b, one + 1].astype(F32)

    def end_scatter(b, ysend, zsend, ys, zs):
        for k in range(nz):
            arrived(ysend.at[b, k], ys.at[b, k])

            @pl.when(z != k)
            def _():
                arrived(zsend.at[b, k], zs.at[b, k])

    def final_in(b, out_ref):
        at = out_rows(b)
        total = scatter_total(b, yrecv2, zrecv2, yr2_s, zr2_s)
        out_ref[at, :] = (base_rows[at, :].astype(F32) + total).astype(BF16)

    def gather_parts(buf, zs, zr, ys, yr):
        def to_partner(c, t, b):
            remote(buf.at[c, b], buf.at[c, b], ys.at[t, b], yr.at[t, b], s, z * 2 + yo).start()

        def by_distance(step):
            def around(k, carry):
                @pl.when(z >= k)
                def _():
                    step(z - k)

                @pl.when(z + k < nz)
                def _():
                    step(z + k)

                return carry

            lax.fori_loop(1, nz, around, 0)

        def along(k, to, c, t, b):
            remote(buf.at[c, b], buf.at[c, b], zs.at[k, b], zr.at[t, b], s, to * 2 + y).start()

        def start(b):
            along(0, jnp.where(at_end, near, outer), g, z, b)
            along(1, mate, g, z, b)
            to_partner(g, z, b)

        def forward(b, use):
            def step(t):
                c = t * 2 + y
                arrived(buf.at[c, b], zr.at[t, b])
                for k, other in ((2, mate), (3, nz - 1 - outer)):

                    @pl.when(jnp.logical_not(at_end) & (t == other))
                    def _():
                        along(k, outer, c, t, b)

                to_partner(c, t, b)
                if use is not None:
                    use(c, b)

            by_distance(step)

        def finish(b, use):
            def step(t):
                c = t * 2 + yo
                arrived(buf.at[c, b], yr.at[t, b])
                if use is not None:
                    use(c, b)

            step(z)
            by_distance(step)

        def end(b):
            for t in range(nz):
                arrived(buf.at[t * 2 + y, b], ys.at[t, b])
            for k in range(2):
                arrived(buf.at[g, b], zs.at[k, b])

            @pl.when(jnp.logical_not(at_end))
            def _():
                for k, other in ((2, mate), (3, nz - 1 - outer)):
                    arrived(buf.at[other * 2 + y, b], zs.at[k, b])

        return start, forward, finish, end

    gather_start, gather_forward, gather_finish, gather_end = gather_parts(
        gath, gz_s, gz_r, gy_s, gy_r
    )
    cot_start, cot_forward, cot_finish, cot_end = gather_parts(cgath, cz_s, cz_r, cy_s, cy_r)
    both = tuple(range(SLOTS))

    def attn_part(b, c):
        return dot(ctx[b], w_out[0, :, chunk_cols(c)]).astype(BF16)

    def back(c):
        part = dot_nt(cgath[c].reshape(rows, cols), w_out[1, :, chunk_cols(c)])
        acc[0] = acc[0] + part.reshape(SLOTS, sub, cols)

    @pl.when(is_enc)
    def _():
        @pl.when(s == 0)
        def _():
            kv_all[:, pl.ds(0, HALO)] = jnp.zeros((2, HALO, cols), BF16)

        @pl.when(is_last)
        def _():
            kv_all[:, pl.ds(HALO + rows, HALO)] = jnp.zeros((2, HALO, cols), BF16)

        load_kv().wait()
        load_q().wait()
        span = sub + 2 * HALO

        def local_block(i):
            def left_halo():
                arrived(kv_all.at[:, pl.ds(0, HALO)], halo_r.at[0])

            def right_halo():
                arrived(kv_all.at[:, pl.ds(HALO + rows, HALO)], halo_r.at[1])

            if i == 0:
                pl.when((s > 0) & (s < enc - 1))(left_halo)
            else:
                pl.when(s < enc - 1)(right_halo)
                pl.when((s > 0) & is_last)(left_halo)
            slot = jnp.where(is_donor, 1 - i, i)
            base = pl.multiple_of(jnp.where(is_last, 1 - i, i) * sub, sub)
            key_pos = s * rows + base - HALO + lax.broadcasted_iota(jnp.int32, (span, 1), 0)
            own_pos = s * rows + base + lax.broadcasted_iota(jnp.int32, (1, sub), 1)
            far = jnp.abs(key_pos - own_pos)
            own_at = pl.ds(pl.multiple_of(s * rows + base, sub), sub)
            in_doc = (key_pos >= bnd_ref[0:1, own_at]) & (key_pos <= bnd_ref[1:2, own_at])
            far_in = jnp.where(in_doc, far, jnp.int32(1 << 20))
            q_at = pl.ds(base, sub)
            k_at = pl.ds(base, span)

            def local_pair(p, carry):
                at = pair_cols(p)
                q_pair = q_own[q_at, at]
                k_pair = kv_all[0, k_at, at]
                v_t = kv_all[1, k_at, at].T
                got = []
                for j in range(2):
                    sc = dot_nt(k_pair, q_pair * lane_masks[j]) * scale
                    sc = jnp.where(far_in <= win_ref[p * 2 + j], sc, LOW)
                    e = jnp.exp(sc - jnp.max(sc, axis=0, keepdims=True))
                    inv = 1.0 / jnp.sum(e, axis=0, keepdims=True)
                    got.append(dot(v_t, (e * inv).astype(BF16)))
                ctx[slot, :, at] = jnp.where(low_row, got[0], got[1]).T.astype(BF16)
                return carry

            lax.fori_loop(0, pairs, local_pair, 0)

        pl.when(s != donor)(functools.partial(local_block, 0))
        pl.semaphore_wait(barrier, slabs + nz - 1)

        @pl.when(s + 1 < enc)
        def _():
            remote(
                kv_ref.at[:, pl.ds(rows - HALO, HALO)],
                kv_all.at[:, pl.ds(0, HALO)],
                halo_s.at[0],
                halo_r.at[0],
                s + 1,
                g,
            ).start()

        @pl.when(s > 0)
        def _():
            remote(
                kv_ref.at[:, pl.ds(0, HALO)],
                kv_all.at[:, pl.ds(HALO + rows, HALO)],
                halo_s.at[1],
                halo_r.at[1],
                s - 1,
                g,
            ).start()

        @pl.when(is_donor)
        def _():
            local_block(0)

        load_wo(0).wait()

        @pl.when(is_donor)
        def _():
            remote(ctx.at[1], ctx.at[1], hand_s.at[1], hand_r.at[1], enc, g).start()
            remote(
                res_ref.at[pl.ds(block_at(1), sub)], slot_res.at[1], hand_s.at[0], hand_r.at[0], enc, g
            ).start()

        @pl.when(s != donor)
        def _():
            scatter_out(0, attn_part, ysend, yrecv, ys_s, yr_s)

        local_block(1)

        @pl.when(is_donor)
        def _():
            scatter_out(0, attn_part, ysend, yrecv, ys_s, yr_s)

    @pl.when(is_dec)
    def _():
        acc[0] = jnp.zeros_like(acc[0])
        pl.semaphore_wait(barrier, slabs + nz - 1)
        for b in both:
            load_cot(b).wait()
            cot_start(b)
        load_wo(0).wait()
        arrived(ctx.at[1], hand_r.at[1])

    @when_has(1)
    def _():
        scatter_out(1, attn_part, ysend, yrecv, ys_s, yr_s)

    @pl.when(is_dec)
    def _():
        load_dq().wait()
        for k in range(enc):
            remote(dq, dq, dq_s.at[k], dq_r, k, g).start()
        for b in both:
            cot_forward(b, None)

    @when_has(0)
    def _():
        scatter_own(0, attn_part)

    @when_has(1)
    def _():
        scatter_own(1, attn_part)

    def start_block(b):
        total = scatter_total(b, yrecv, zrecv, yr_s, zr_s)
        hidden = (slot_res[b].astype(F32) + total).astype(BF16)
        gath[g, b] = hidden
        gather_start(b)

        @pl.when(is_enc)
        def _():
            states_ref[out_rows(b), :] = hidden

    def project(c, b):
        block = gath[c, b]
        acc[0, b] = acc[0, b] + dot(block, w_kv[0, chunk_cols(c), :])
        acc[1, b] = acc[1, b] + dot(block, w_kv[1, chunk_cols(c), :])

    def project_own(b):
        block = gath[g, b]
        acc[0, b] = dot(block, w_kv[0, chunk_cols(g), :])
        acc[1, b] = dot(block, w_kv[1, chunk_cols(g), :])

    @when_has(0)
    def _():
        scatter_join(0, yrecv, zsend, zrecv, yr_s, zs_s, zr_s)

    @when_has(1)
    def _():
        scatter_join(1, yrecv, zsend, zrecv, yr_s, zs_s, zr_s)

    @when_has(0)
    def _():
        load_res(0).wait()
        start_block(0)

    @when_has(1)
    def _():
        @pl.when(is_enc)
        def _():
            load_res(1).wait()

        @pl.when(is_dec)
        def _():
            arrived(slot_res.at[1], hand_r.at[0])

        start_block(1)

        @pl.when(is_dec)
        def _():
            remote(gath.at[g, 1], back_rows, hand_s.at[0], hand_r.at[2], donor, g).start()


    @pl.when(is_dec)
    def _():
        load_wo(1).wait()

        def near(k, carry):
            back(k * 2 + y)
            return carry

        lax.fori_loop(0, nz, near, 0)
        for b in both:
            cot_finish(b, None)

        def over(k, carry):
            back(k * 2 + yo)
            return carry

        lax.fori_loop(0, nz, over, 0)
        for b in both:
            dg[b * sub : (b + 1) * sub, :] = acc[0, b].astype(BF16)
        for k in range(enc):
            remote(dg, dg, dg_s.at[k], dg_r, k, g).start()

    load_wkv().wait()

    @when_has(0)
    def _():
        project_own(0)
        gather_forward(0, project)

    @when_has(1)
    def _():
        project_own(1)
        gather_forward(1, project)

    for b in both:

        @pl.when(jnp.logical_not(has[b]))
        def _():
            stat[b, 0] = jnp.full((heads, rows), LOW, F32)
            stat[b, 1] = jnp.zeros((heads, rows), F32)
            stat[b, 2] = jnp.zeros((heads, rows), F32)
            ctx_acc[b] = jnp.zeros((cols, rows), F32)

    @pl.when(jnp.logical_not(has[0]))
    def _():
        q_acc[...] = jnp.zeros((cols, rows), F32)

    def cross_block(b):
        for i in range(2):
            kv_new[b, i] = acc[i, b].astype(BF16)
        tok_pos = key_base(b) + lax.broadcasted_iota(jnp.int32, (sub, 1), 0)
        seen = (tok_pos >= bnd_ref[0:1, enc * rows :]) & (tok_pos <= bnd_ref[1:2, enc * rows :])

        def cross_pair(p, carry):
            at = pair_cols(p)
            q_pair = dq[:, at]
            g_pair = dg[:, at]
            k_pair = kv_new[b, 0, :, at]
            v_pair = kv_new[b, 1, :, at]
            v_t = v_pair.T
            got = []
            for i in range(2):
                sc = dot_nt(k_pair, q_pair * lane_masks[i]) * scale
                sc = jnp.where(seen, sc, LOW)
                top = jnp.max(sc, axis=0, keepdims=True)
                e = jnp.exp(sc - top)
                dp = dot_nt(v_pair, g_pair * lane_masks[i])
                h = p * 2 + i
                e_buf[b, h] = e
                d_buf[b, h] = dp
                stat[b, 0, pl.ds(h, 1), :] = top
                stat[b, 1, pl.ds(h, 1), :] = jnp.sum(e, axis=0, keepdims=True)
                stat[b, 2, pl.ds(h, 1), :] = jnp.sum(e * dp, axis=0, keepdims=True)
                got.append(dot(v_t, e.astype(BF16)))
            ctx_acc[b, pair_cols(p), :] = jnp.where(low_row, got[0], got[1])
            return carry

        lax.fori_loop(0, pairs, cross_pair, 0)

    @when_has(0)
    def _():
        gather_finish(0, project)
        arrived(dq, dq_r)
        arrived(dg, dg_r)
        cross_block(0)

    @when_has(1)
    def _():
        gather_finish(1, project)
        cross_block(1)

    own_top = jnp.maximum(stat[0, 0], stat[1, 0])
    lift = [jnp.exp(stat[b, 0] - own_top) for b in both]
    stat_all[s, 0] = own_top
    stat_all[s, 1] = lift[0] * stat[0, 1] + lift[1] * stat[1, 1]
    stat_all[s, 2] = lift[0] * stat[0, 2] + lift[1] * stat[1, 2]
    for k in range(1, slabs):
        to = lax.rem(s + k, slabs)
        remote(stat_all.at[s], stat_all.at[s], st_s.at[k - 1], st_r.at[s], to, g).start()
    for h in range(heads):
        at = slice(h * HD, (h + 1) * HD)
        tbuf[at, :] = (
            lift[0][h : h + 1, :] * ctx_acc[0, at, :] + lift[1][h : h + 1, :] * ctx_acc[1, at, :]
        ).astype(BF16)

    @pl.when(is_enc)
    def _():
        remote(tbuf, ctx_in.at[s], cx_s, cx_r.at[s], enc, g).start()

    for k in range(1, slabs):
        at = lax.rem(s + k, slabs)
        arrived(stat_all.at[at], st_r.at[at])
    top = stat_all[0, 0]
    for i in range(1, slabs):
        top = jnp.maximum(top, stat_all[i, 0])
    shifts = [jnp.exp(stat_all[i, 0] - top) for i in range(slabs)]
    total = shifts[0] * stat_all[0, 1]
    dots = shifts[0] * stat_all[0, 2]
    for i in range(1, slabs):
        total = total + shifts[i] * stat_all[i, 1]
        dots = dots + shifts[i] * stat_all[i, 2]
    inv_total = 1.0 / total
    for b in both:
        fac[b] = jnp.exp(stat[b, 0] - top) * inv_total
    fac[SLOTS] = dots * inv_total

    def grad_block(b):
        def grad_pair(p, carry):
            at = pair_cols(p)
            q_pair = dq[:, at]
            g_pair = dg[:, at]
            k_t = kv_new[b, 0, :, at].T
            kg, vg, qg = [], [], []
            for i in range(2):
                h = p * 2 + i
                w = e_buf[b, h] * fac[b, pl.ds(h, 1), :]
                ds = (w * (d_buf[b, h] - fac[SLOTS, pl.ds(h, 1), :])).astype(BF16)
                vg.append(dot(w.astype(BF16), g_pair))
                kg.append(dot(ds, q_pair))
                qg.append(dot(k_t, ds))
            kvg[b, 0, :, at] = (scale * jnp.where(low_lane, kg[0], kg[1])).astype(BF16)
            kvg[b, 1, :, at] = jnp.where(low_lane, vg[0], vg[1]).astype(BF16)
            mine = scale * jnp.where(low_row, qg[0], qg[1])
            q_acc[pair_cols(p), :] = mine if b == 0 else q_acc[pair_cols(p), :] + mine
            return carry

        lax.fori_loop(0, pairs, grad_pair, 0)

    def grad_part(b, c):
        return (
            dot_nt(kvg[b, 0], w_kv[0, chunk_cols(c), :]) + dot_nt(kvg[b, 1], w_kv[1, chunk_cols(c), :])
        ).astype(BF16)

    def final_out(b, part):
        scatter_out(b, part, ysend2, yrecv2, ys2_s, yr2_s)

    @when_has(0)
    def _():
        grad_block(0)
        final_out(0, grad_part)

    @when_has(1)
    def _():
        grad_block(1)

    @pl.when(is_enc)
    def _():
        qg_buf[...] = q_acc[...].astype(BF16)

        @pl.when(is_donor)
        def _():
            scatter_own(0, grad_part)
            arrived(kvg.at[1], hand_r.at[3])

        final_out(1, grad_part)
        remote(qg_buf, qg_in.at[s], qg_s, qg_r.at[s], enc, g).start()

        @pl.when(s != donor)
        def _():
            scatter_own(0, grad_part)

        scatter_own(1, grad_part)
        load_base(cot_ref).wait()
        for b in both:
            scatter_join(b, yrecv2, zsend2, zrecv2, yr2_s, zs2_s, zr2_s)
        for b in both:
            final_in(b, grads_ref)

        @pl.when(is_donor)
        def _():
            arrived(back_rows, hand_r.at[2])
            states_ref[out_rows(1), :] = back_rows[...]
            arrived(slot_res.at[1], hand_s.at[0])
            arrived(ctx.at[1], hand_s.at[1])
            load_res(1).wait()

        @pl.when(s + 1 < enc)
        def _():
            arrived(kv_ref.at[:, pl.ds(rows - HALO, HALO)], halo_s.at[0])

        @pl.when(s > 0)
        def _():
            arrived(kv_ref.at[:, pl.ds(0, HALO)], halo_s.at[1])

        arrived(tbuf, cx_s)
        arrived(qg_buf, qg_s)

    @pl.when(is_dec)
    def _():
        remote(kvg.at[1], kvg.at[1], hand_s.at[1], hand_r.at[3], donor, g).start()
        ctx_in[enc] = tbuf[...]
        for k in range(enc):
            arrived(ctx_in.at[k], cx_r.at[k])
        shares = [shifts[k] * inv_total for k in range(slabs)]
        for p in range(pairs):
            mixed = []
            for h in (2 * p, 2 * p + 1):
                at = slice(h * HD, (h + 1) * HD)
                part = shares[0][h : h + 1, :] * ctx_in[0, at, :].astype(F32)
                for k in range(1, slabs):
                    part = part + shares[k][h : h + 1, :] * ctx_in[k, at, :].astype(F32)
                mixed.append(part)
            dctx[:, p * PAIR : (p + 1) * PAIR] = jnp.concatenate(mixed, axis=0).T.astype(BF16)

        def dec_part(b, c):
            return dot(dctx[b * sub : (b + 1) * sub, :], w_out[1, :, chunk_cols(c)]).astype(BF16)

        for b in both:
            final_out(b, dec_part)
        for b in both:
            scatter_own(b, dec_part)
        load_base(res_ref).wait()
        for b in both:
            scatter_join(b, yrecv2, zsend2, zrecv2, yr2_s, zs2_s, zr2_s)
        for k in range(enc):
            arrived(qg_in.at[k], qg_r.at[k])
        for p in range(pairs):
            at = slice(p * PAIR, (p + 1) * PAIR)
            part = q_acc[at, :]
            for k in range(enc):
                part = part + qg_in[k, at, :].astype(F32)
            grads_ref[:, at] = part.T.astype(BF16)
        for b in both:
            final_in(b, states_ref)
        for k in range(enc):
            arrived(dq, dq_s.at[k])
            arrived(dg, dg_s.at[k])
        for b in both:
            cot_end(b)
        arrived(gath.at[g, 1], hand_s.at[0])
        arrived(kvg.at[1], hand_s.at[1])

    for b in both:

        @when_has(b)
        def _():
            end_scatter(b, ysend, zsend, ys_s, zs_s)
            gather_end(b)

        end_scatter(b, ysend2, zsend2, ys2_s, zs2_s)
    for k in range(1, slabs):
        arrived(stat_all.at[s], st_s.at[k - 1])


def deliver(states_in, grads_in, states_out, grads_out):
    states_out[...] = states_in[...]
    grads_out[...] = grads_in[...]


def layer(slabs, groups, queries, keys_values, residual, cotangent, out_weight, kv_weight, bounds, windows):
    rows, cols = queries.shape
    heads = cols // HD
    nz = groups // 2
    enc = slabs - 1
    sub = rows // SLOTS
    width = out_weight.shape[2]
    dma = pltpu.SemaphoreType.DMA
    parts = lambda: pltpu.VMEM((SLOTS, nz, sub, cols), BF16)
    vmem = pl.BlockSpec(memory_space=pltpu.VMEM)
    hbm = pl.BlockSpec(memory_space=pl.ANY)
    states, grads = pl.pallas_call(
        functools.partial(layer_kernel, slabs, groups),
        out_shape=(jax.ShapeDtypeStruct((rows, cols), BF16),) * 2,
        in_specs=[hbm] * 6 + [vmem, pl.BlockSpec(memory_space=pltpu.SMEM)],
        out_specs=(vmem, vmem),
        scratch_shapes=[
            pltpu.VMEM((2, cols, width), BF16),
            pltpu.VMEM((2, width, cols), BF16),
            pltpu.VMEM((2, rows + 2 * HALO, cols), BF16),
            pltpu.VMEM((rows, cols), BF16),
            pltpu.VMEM((rows, cols), BF16),
            pltpu.VMEM((SLOTS, sub, cols), BF16),
            pltpu.VMEM((SLOTS, sub, cols), BF16),
        ]
        + [parts() for _ in range(9)]
        + [
            pltpu.VMEM((groups, SLOTS, sub, cols), BF16),
            pltpu.VMEM((groups, SLOTS, sub, cols), BF16),
            pltpu.VMEM((2, SLOTS, sub, cols), F32),
            pltpu.VMEM((SLOTS, 2, sub, cols), BF16),
            pltpu.VMEM((rows, cols), BF16),
            pltpu.VMEM((rows, cols), BF16),
            pltpu.VMEM((SLOTS, heads, sub, rows), F32),
            pltpu.VMEM((SLOTS, heads, sub, rows), F32),
            pltpu.VMEM((SLOTS, 3, heads, rows), F32),
            pltpu.VMEM((SLOTS, cols, rows), F32),
            pltpu.VMEM((slabs, 3, heads, rows), F32),
            pltpu.VMEM((SLOTS + 1, heads, rows), F32),
            pltpu.VMEM((cols, rows), BF16),
            pltpu.VMEM((slabs, cols, rows), BF16),
            pltpu.VMEM((cols, rows), F32),
            pltpu.VMEM((cols, rows), BF16),
            pltpu.VMEM((enc, cols, rows), BF16),
            pltpu.VMEM((SLOTS, 2, sub, cols), BF16),
            pltpu.VMEM((rows, cols), BF16),
            pltpu.VMEM((sub, cols), BF16),
            dma((3,)),
            dma((5,)),
            dma((2,)),
            dma((2,)),
        ]
        + [dma((SLOTS, nz))] * 8
        + [dma((nz, SLOTS))] * 8
        + [
            dma((enc,)),
            dma,
            dma((enc,)),
            dma,
            dma((enc,)),
            dma((slabs,)),
            dma,
            dma((enc,)),
            dma,
            dma((enc,)),
            dma((2,)),
            dma((4,)),
        ],
        compiler_params=pltpu.CompilerParams(
            collective_id=0, has_side_effects=True, vmem_limit_bytes=60 * 1024 * 1024
        ),
    )(queries, keys_values, residual, cotangent, out_weight, kv_weight, bounds, windows)
    return pl.pallas_call(
        deliver,
        out_shape=(jax.ShapeDtypeStruct((rows, cols), BF16),) * 2,
        in_specs=[vmem] * 2,
        out_specs=(vmem, vmem),
    )(states, grads)


def one_decoder_slab(mesh):
    slabs, groups = mesh.shape["seq"], mesh.shape["mp"]
    return slabs == 4 and groups == 8


def solution(mesh):
    body = shards
    if one_decoder_slab(mesh):
        body = functools.partial(layer, mesh.shape["seq"], mesh.shape["mp"])

    return jax.shard_map(
        body,
        mesh=mesh,
        in_specs=(
            P("seq", "mp"),
            P(None, "seq", "mp"),
            P("seq", "mp"),
            P("seq", "mp"),
            P(None, "mp", None),
            P(None, None, "mp"),
            P(),
            P("mp"),
        ),
        out_specs=(P("seq", "mp"), P("seq", "mp")),
        check_vma=False,
    )
```

```python
import functools

import jax
import jax.numpy as jnp
from jax import lax
from jax.experimental import pallas as pl
from jax.experimental.pallas import tpu as pltpu
from jax.sharding import PartitionSpec as P

HD = 64
WIN = 127


def with_halo(cells, sides, width):
    for axis, dim in sides:
        count = lax.axis_size(axis)
        ends = count - 1
        head = lax.slice_in_dim(cells, 0, width, axis=dim)
        tail = lax.slice_in_dim(cells, cells.shape[dim] - width, cells.shape[dim], axis=dim)
        cells = jnp.concatenate(
            [
                lax.ppermute(tail, axis, [(i, (i + 1) % count) for i in range(ends)]),
                cells,
                lax.ppermute(head, axis, [((i + 1) % count, i) for i in range(ends)]),
            ],
            axis=dim,
        )
    return cells


def softmax_masked(scores, permitted):
    masked_scores = jnp.where(permitted, scores, -jnp.inf)
    row_top = jnp.max(masked_scores, axis=-1, keepdims=True)
    exp_scores = jnp.exp(masked_scores - row_top)
    return exp_scores / jnp.sum(exp_scores, axis=-1, keepdims=True)


def shards(queries, keys_values, residual, cotangent, out_weight, kv_weight, bounds, windows):
    row_count = queries.shape[0]
    col_count = queries.shape[1]
    head_count = col_count // HD
    slab_count = lax.axis_size("seq")
    enc_slabs = 3 * slab_count // 4
    dec_slabs = slab_count - enc_slabs
    enc_tokens = enc_slabs * row_count
    token_count = slab_count * row_count
    dec_tokens = token_count - enc_tokens
    slab_index = lax.axis_index("seq")
    is_enc = slab_index < enc_slabs
    score_scale = HD ** (-0.5)
    own_pos = slab_index * row_count + jnp.arange(row_count, dtype=jnp.int32)
    own_first = lax.dynamic_slice_in_dim(bounds[0], slab_index * row_count, row_count)
    own_last = lax.dynamic_slice_in_dim(bounds[1], slab_index * row_count, row_count)
    query_heads = queries.reshape(row_count, head_count, HD)
    slice_cols = residual.shape[1]
    res_full, cot_full = (
        lax.all_gather(residual, "mp", axis=1, tiled=True),
        lax.all_gather(cotangent, "mp", axis=1, tiled=True),
    )
    model_width = cot_full.shape[1]
    rim_keys = with_halo(keys_values, (("seq", 1),), WIN)

    def local_part():
        span_count = rim_keys.shape[1]
        key_pos = slab_index * row_count - WIN + jnp.arange(span_count, dtype=jnp.int32)
        key_heads = rim_keys[0].reshape(span_count, head_count, HD)
        value_heads = rim_keys[1].reshape(span_count, head_count, HD)
        scores = (
            jnp.einsum("qhd,khd->hqk", query_heads, key_heads, preferred_element_type=jnp.float32)
            * score_scale
        )
        in_document = (key_pos[None, :] >= own_first[:, None]) & (
            key_pos[None, :] <= own_last[:, None]
        )
        distance = jnp.abs(own_pos[:, None] - key_pos[None, :])
        permitted = in_document[None] & (distance[None] <= windows[:, None, None])
        rounded = softmax_masked(scores, permitted).astype(jnp.bfloat16)
        context = jnp.einsum(
            "hqk,khd->qhd", rounded, value_heads, preferred_element_type=jnp.float32
        ).astype(jnp.bfloat16)
        return jnp.dot(
            context.reshape(row_count, col_count), out_weight[0], preferred_element_type=jnp.float32
        )

    head_partial = lax.cond(
        is_enc, local_part, lambda: jnp.zeros((row_count, model_width), jnp.float32)
    )
    attn_sum = lax.psum(head_partial.astype(jnp.bfloat16), "mp").astype(jnp.float32)
    hidden_full = (res_full.astype(jnp.float32) + attn_sum).astype(jnp.bfloat16)
    encoder_out = lax.dynamic_slice_in_dim(
        hidden_full, lax.axis_index("mp") * slice_cols, slice_cols, 1
    )

    def project_keys():
        key_proj = jnp.dot(hidden_full, kv_weight[0], preferred_element_type=jnp.float32).astype(
            jnp.bfloat16
        )
        value_proj = jnp.dot(hidden_full, kv_weight[1], preferred_element_type=jnp.float32).astype(
            jnp.bfloat16
        )
        return jnp.stack([key_proj, value_proj])

    cross_kv = lax.cond(
        is_enc, project_keys, lambda: jnp.zeros((2, row_count, col_count), jnp.bfloat16)
    )

    def context_gradient():
        return lax.dot_general(
            cot_full, out_weight[1], (((1,), (1,)), ((), ())), preferred_element_type=jnp.float32
        ).astype(jnp.bfloat16)

    dec_queries = lax.all_gather(queries, "seq", axis=0, tiled=True)[enc_tokens:]
    dec_heads = dec_queries.reshape(dec_tokens, head_count, HD)
    dec_first = bounds[0, enc_tokens:]
    dec_last = bounds[1, enc_tokens:]
    in_document = (own_pos[None, :] >= dec_first[:, None]) & (own_pos[None, :] <= dec_last[:, None])
    key_heads = cross_kv[0].reshape(row_count, head_count, HD)
    value_heads = cross_kv[1].reshape(row_count, head_count, HD)
    scores = (
        jnp.einsum("qhd,khd->hqk", dec_heads, key_heads, preferred_element_type=jnp.float32)
        * score_scale
    )
    masked_scores = jnp.where(in_document[None], scores, -jnp.inf)
    row_top = lax.pmax(jnp.max(masked_scores, axis=2), "seq")
    exp_scores = jnp.exp(masked_scores - row_top[:, :, None])
    row_total = lax.psum(jnp.sum(exp_scores, axis=2), "seq")
    weights = exp_scores / row_total[:, :, None]
    rounded = weights.astype(jnp.bfloat16)
    partial_ctx = jnp.einsum(
        "hqk,khd->qhd", rounded, value_heads, preferred_element_type=jnp.float32
    ).reshape(dec_tokens, col_count)
    context_all = lax.psum(partial_ctx.astype(jnp.bfloat16), "seq")
    dec_offset = jnp.maximum(slab_index - enc_slabs, 0) * row_count
    context = lax.dynamic_slice_in_dim(context_all, dec_offset, row_count, 0)
    out_part = lax.cond(
        is_enc,
        lambda: jnp.zeros((row_count, model_width), jnp.float32),
        lambda: jnp.dot(context, out_weight[1], preferred_element_type=jnp.float32),
    )
    grad_own = lax.cond(
        is_enc, lambda: jnp.zeros((row_count, col_count), jnp.bfloat16), context_gradient
    )
    grad_all = lax.all_gather(grad_own, "seq", axis=0, tiled=True)[enc_tokens:]
    grad_heads = grad_all.reshape(dec_tokens, head_count, HD)
    row_dots = jnp.einsum(
        "qhd,qhd->hq",
        grad_heads,
        context_all.reshape(dec_tokens, head_count, HD),
        preferred_element_type=jnp.float32,
    )
    prob_grad = jnp.einsum(
        "qhd,khd->hqk", grad_heads, value_heads, preferred_element_type=jnp.float32
    )
    score_grad = (weights * (prob_grad - row_dots[:, :, None])).astype(jnp.bfloat16)
    grad_blocks = score_grad.reshape(head_count, dec_slabs, row_count, row_count)
    prob_blocks = rounded.reshape(head_count, dec_slabs, row_count, row_count)
    query_blocks = dec_heads.reshape(dec_slabs, row_count, head_count, HD)
    grad_rows = grad_heads.reshape(dec_slabs, row_count, head_count, HD)
    key_parts = (
        score_scale
        * jnp.einsum(
            "hsqk,sqhd->skhd", grad_blocks, query_blocks, preferred_element_type=jnp.float32
        )
    ).astype(jnp.bfloat16)
    value_parts = jnp.einsum(
        "hsqk,sqhd->skhd", prob_blocks, grad_rows, preferred_element_type=jnp.float32
    ).astype(jnp.bfloat16)
    key_grad = (
        jnp.sum(key_parts.astype(jnp.float32), axis=0)
        .astype(jnp.bfloat16)
        .reshape(row_count, col_count)
    )
    value_grad = (
        jnp.sum(value_parts.astype(jnp.float32), axis=0)
        .astype(jnp.bfloat16)
        .reshape(row_count, col_count)
    )
    query_terms = score_scale * jnp.einsum(
        "hqk,khd->qhd", score_grad, key_heads, preferred_element_type=jnp.float32
    )
    query_sum = lax.psum(
        query_terms.reshape(dec_tokens, col_count).astype(jnp.bfloat16), "seq"
    ).astype(jnp.float32)
    query_grad = lax.dynamic_slice_in_dim(query_sum, dec_offset, row_count, 0).astype(jnp.bfloat16)
    contract = (((1,), (1,)), ((), ()))
    grad_terms = lax.dot_general(
        key_grad, kv_weight[0], contract, preferred_element_type=jnp.float32
    ) + lax.dot_general(value_grad, kv_weight[1], contract, preferred_element_type=jnp.float32)
    final_term = jnp.where(is_enc, grad_terms, out_part)
    final_share = lax.psum_scatter(
        final_term.astype(jnp.bfloat16), "mp", scatter_dimension=1, tiled=True
    ).astype(jnp.float32)
    base_rows = jnp.where(is_enc, cotangent, residual).astype(jnp.float32)
    final_rows = (base_rows + final_share).astype(jnp.bfloat16)
    states_out = jnp.where(is_enc, encoder_out, final_rows)
    grad_states = jnp.where(is_enc, final_rows, query_grad)
    return (states_out, grad_states)


F32 = jnp.float32
BF16 = jnp.bfloat16
LOW = -1e30
PAIR = 2 * HD
HALO = 128
SLOTS = 2
NT = (((1,), (1,)), ((), ()))


def dot(a, b):
    return jnp.dot(a, b, preferred_element_type=F32)


def dot_nt(a, b):
    return lax.dot_general(a, b, NT, preferred_element_type=F32)


def layer_kernel(
    slabs,
    groups,
    q_ref,
    kv_ref,
    res_ref,
    cot_ref,
    ow_ref,
    kw_ref,
    bnd_ref,
    win_ref,
    states_ref,
    grads_ref,
    w_out,
    w_kv,
    kv_all,
    q_own,
    base_rows,
    slot_res,
    ctx,
    own_part,
    ysend,
    yrecv,
    zsend,
    zrecv,
    ysend2,
    yrecv2,
    zsend2,
    zrecv2,
    gath,
    cgath,
    acc,
    kv_new,
    dq,
    dg,
    e_buf,
    d_buf,
    stat,
    ctx_acc,
    stat_all,
    fac,
    tbuf,
    ctx_in,
    q_acc,
    qg_buf,
    qg_in,
    kvg,
    dctx,
    back_rows,
    w_sem,
    in_sem,
    halo_s,
    halo_r,
    ys_s,
    yr_s,
    zs_s,
    zr_s,
    ys2_s,
    yr2_s,
    zs2_s,
    zr2_s,
    gz_s,
    gz_r,
    gy_s,
    gy_r,
    cz_s,
    cz_r,
    cy_s,
    cy_r,
    dq_s,
    dq_r,
    dg_s,
    dg_r,
    st_s,
    st_r,
    cx_s,
    cx_r,
    qg_s,
    qg_r,
    hand_s,
    hand_r,
):
    rows, cols = q_own.shape
    pairs = cols // PAIR
    heads = cols // HD
    enc = slabs - 1
    donor = enc // 2
    sub = rows // SLOTS
    nz = groups // 2
    scale = HD ** (-0.5)
    s = lax.axis_index("seq")
    g = lax.axis_index("mp")
    z = g // 2
    y = lax.rem(g, 2)
    yo = 1 - y
    low = z < nz // 2
    at_end = (z == 0) | (z == nz - 1)
    outer = jnp.where(low, 0, nz - 1)
    near = jnp.where(low, 1, nz - 2)
    mate = nz - 1 - near

    def remote(src, dst, send, recv, seq, mp):
        return pltpu.make_async_remote_copy(
            src_ref=src,
            dst_ref=dst,
            send_sem=send,
            recv_sem=recv,
            device_id={"seq": seq, "mp": mp},
            device_id_type=pl.DeviceIdType.MESH,
        )

    def arrived(dst, recv):
        pltpu.make_async_copy(dst, dst, recv).wait()

    is_enc = s < enc
    is_dec = s >= enc
    is_donor = s == donor
    is_last = s == enc - 1
    has = (is_enc, s != donor)

    def when_has(b):
        return pl.when(has[b])

    def block_at(b):
        return pl.multiple_of(jnp.where(is_donor | is_last, 1 - b, b) * sub, sub)

    def out_rows(b):
        return pl.ds(pl.multiple_of(jnp.where(is_dec, b * sub, block_at(b)), sub), sub)

    def key_base(b):
        return jnp.where(is_dec, donor * rows, s * rows + block_at(b))

    def load_q():
        return pltpu.make_async_copy(q_ref, q_own, in_sem.at[0])

    def load_kv():
        return pltpu.make_async_copy(kv_ref, kv_all.at[:, pl.ds(HALO, rows)], in_sem.at[1])

    def load_res(b):
        return pltpu.make_async_copy(res_ref.at[pl.ds(block_at(b), sub)], slot_res.at[b], in_sem.at[2 + b])

    def load_base(ref):
        return pltpu.make_async_copy(ref, base_rows, in_sem.at[4])

    def load_cot(b):
        return pltpu.make_async_copy(cot_ref.at[pl.ds(b * sub, sub)], cgath.at[g, b], in_sem.at[2 + b])

    def load_dq():
        return pltpu.make_async_copy(q_ref, dq, in_sem.at[0])

    def load_wo(i):
        return pltpu.make_async_copy(ow_ref.at[i], w_out.at[i], w_sem.at[i])

    def load_wkv():
        return pltpu.make_async_copy(kw_ref, w_kv, w_sem.at[2])

    barrier = pltpu.get_barrier_semaphore()

    def greet(seq, mp):
        pl.semaphore_signal(
            barrier,
            inc=1,
            device_id={"seq": seq, "mp": mp},
            device_id_type=pl.DeviceIdType.MESH,
        )

    for k in range(1, slabs):
        greet(lax.rem(s + k, slabs), g)
    for k in range(1, nz):
        greet(s, lax.rem(z + k, nz) * 2 + y)
    greet(s, z * 2 + yo)

    @pl.when(is_enc)
    def _():
        load_kv().start()
        load_q().start()
        load_wo(0).start()
        for b in range(SLOTS):
            load_res(b).start()
        load_wkv().start()
        load_base(cot_ref).start()

    @pl.when(is_dec)
    def _():
        for b in range(SLOTS):
            load_cot(b).start()
        load_wo(0).start()
        load_wo(1).start()
        load_dq().start()
        load_wkv().start()
        load_base(res_ref).start()

    lane = lax.broadcasted_iota(jnp.int32, (1, PAIR), 1)
    low_lane = lane < HD
    lane_masks = (
        jnp.where(low_lane, 1.0, 0.0).astype(BF16),
        jnp.where(low_lane, 0.0, 1.0).astype(BF16),
    )
    low_row = lax.broadcasted_iota(jnp.int32, (PAIR, 1), 0) < HD

    def pair_cols(p):
        return pl.ds(pl.multiple_of(p * PAIR, PAIR), PAIR)

    def chunk_cols(c):
        return pl.ds(pl.multiple_of(c * cols, cols), cols)

    def nth(k):
        t = jnp.where(at_end, nz - 1 - k, jnp.where(k == 0, 0, nz - k))
        return jnp.where(low, t, nz - 1 - t)

    def scatter_out(b, part, ysend, yrecv, ys, yr):
        def first(k, carry):
            t = nth(k)
            ysend[b, t] = part(b, t * 2 + yo)
            remote(ysend.at[b, t], yrecv.at[b, t], ys.at[b, t], yr.at[b, t], s, z * 2 + yo).start()
            return carry

        lax.fori_loop(0, nz, first, 0)

    def scatter_own(b, part):
        def own(k, carry):
            t = nth(k)
            own_part[b, t] = part(b, t * 2 + y)
            return carry

        lax.fori_loop(0, nz, own, 0)

    def scatter_join(b, yrecv, zsend, zrecv, yr, zs, zr):
        def second(k, carry):
            t = nth(k)
            arrived(yrecv.at[b, t], yr.at[b, t])
            joined = own_part[b, t].astype(F32) + yrecv[b, t].astype(F32)

            @pl.when(at_end | (t == outer))
            def _():
                zsend[b, t] = joined.astype(BF16)

            @pl.when(jnp.logical_not(at_end | (t == outer)))
            def _():
                arrived(zrecv.at[b, t], zr.at[b, t])
                zsend[b, t] = (joined + zrecv[b, t].astype(F32)).astype(BF16)

            to = jnp.where(at_end, near, t)
            slot = jnp.where(at_end, t, jnp.where(t == mate, nz - 1 - outer, z))
            remote(
                zsend.at[b, t], zrecv.at[b, slot], zs.at[b, t], zr.at[b, slot], s, to * 2 + y
            ).start()
            return carry

        lax.fori_loop(0, nz - 1, second, 0)

    def scatter_total(b, yrecv, zrecv, yr, zr):
        arrived(yrecv.at[b, z], yr.at[b, z])
        one = jnp.where(at_end, 1, jnp.where(low, 0, nz - 2))
        for k in range(2):
            arrived(zrecv.at[b, one + k], zr.at[b, one + k])
        total = own_part[b, z].astype(F32) + yrecv[b, z].astype(F32)
        return total + zrecv[b, one].astype(F32) + zrecv[b, one + 1].astype(F32)

    def end_scatter(b, ysend, zsend, ys, zs):
        for k in range(nz):
            arrived(ysend.at[b, k], ys.at[b, k])

            @pl.when(z != k)
            def _():
                arrived(zsend.at[b, k], zs.at[b, k])

    def final_in(b, out_ref):
        at = out_rows(b)
        total = scatter_total(b, yrecv2, zrecv2, yr2_s, zr2_s)
        out_ref[at, :] = (base_rows[at, :].astype(F32) + total).astype(BF16)

    def gather_parts(buf, zs, zr, ys, yr):
        def to_partner(c, t, b):
            remote(buf.at[c, b], buf.at[c, b], ys.at[t, b], yr.at[t, b], s, z * 2 + yo).start()

        def by_distance(step):
            def around(k, carry):
                @pl.when(z >= k)
                def _():
                    step(z - k)

                @pl.when(z + k < nz)
                def _():
                    step(z + k)

                return carry

            lax.fori_loop(1, nz, around, 0)

        def along(k, to, c, t, b):
            remote(buf.at[c, b], buf.at[c, b], zs.at[k, b], zr.at[t, b], s, to * 2 + y).start()

        def start(b):
            along(0, jnp.where(at_end, near, outer), g, z, b)
            along(1, mate, g, z, b)
            to_partner(g, z, b)

        def forward(b, use):
            def step(t):
                c = t * 2 + y
                arrived(buf.at[c, b], zr.at[t, b])
                for k, other in ((2, mate), (3, nz - 1 - outer)):

                    @pl.when(jnp.logical_not(at_end) & (t == other))
                    def _():
                        along(k, outer, c, t, b)

                to_partner(c, t, b)
                if use is not None:
                    use(c, b)

            by_distance(step)

        def finish(b, use):
            def step(t):
                c = t * 2 + yo
                arrived(buf.at[c, b], yr.at[t, b])
                if use is not None:
                    use(c, b)

            step(z)
            by_distance(step)

        def end(b):
            for t in range(nz):
                arrived(buf.at[t * 2 + y, b], ys.at[t, b])
            for k in range(2):
                arrived(buf.at[g, b], zs.at[k, b])

            @pl.when(jnp.logical_not(at_end))
            def _():
                for k, other in ((2, mate), (3, nz - 1 - outer)):
                    arrived(buf.at[other * 2 + y, b], zs.at[k, b])

        return start, forward, finish, end

    gather_start, gather_forward, gather_finish, gather_end = gather_parts(
        gath, gz_s, gz_r, gy_s, gy_r
    )
    cot_start, cot_forward, cot_finish, cot_end = gather_parts(cgath, cz_s, cz_r, cy_s, cy_r)
    both = tuple(range(SLOTS))

    def attn_part(b, c):
        return dot(ctx[b], w_out[0, :, chunk_cols(c)]).astype(BF16)

    def back(c):
        part = dot_nt(cgath[c].reshape(rows, cols), w_out[1, :, chunk_cols(c)])
        acc[0] = acc[0] + part.reshape(SLOTS, sub, cols)

    @pl.when(is_enc)
    def _():
        @pl.when(s == 0)
        def _():
            kv_all[:, pl.ds(0, HALO)] = jnp.zeros((2, HALO, cols), BF16)

        @pl.when(is_last)
        def _():
            kv_all[:, pl.ds(HALO + rows, HALO)] = jnp.zeros((2, HALO, cols), BF16)

        load_kv().wait()
        load_q().wait()
        span = sub + 2 * HALO

        def local_block(i):
            def left_halo():
                arrived(kv_all.at[:, pl.ds(0, HALO)], halo_r.at[0])

            def right_halo():
                arrived(kv_all.at[:, pl.ds(HALO + rows, HALO)], halo_r.at[1])

            if i == 0:
                pl.when((s > 0) & (s < enc - 1))(left_halo)
            else:
                pl.when(s < enc - 1)(right_halo)
                pl.when((s > 0) & is_last)(left_halo)
            slot = jnp.where(is_donor, 1 - i, i)
            base = pl.multiple_of(jnp.where(is_last, 1 - i, i) * sub, sub)
            key_pos = s * rows + base - HALO + lax.broadcasted_iota(jnp.int32, (span, 1), 0)
            own_pos = s * rows + base + lax.broadcasted_iota(jnp.int32, (1, sub), 1)
            far = jnp.abs(key_pos - own_pos)
            own_at = pl.ds(pl.multiple_of(s * rows + base, sub), sub)
            in_doc = (key_pos >= bnd_ref[0:1, own_at]) & (key_pos <= bnd_ref[1:2, own_at])
            far_in = jnp.where(in_doc, far, jnp.int32(1 << 20))
            q_at = pl.ds(base, sub)
            k_at = pl.ds(base, span)

            def local_pair(p, carry):
                at = pair_cols(p)
                q_pair = q_own[q_at, at]
                k_pair = kv_all[0, k_at, at]
                v_t = kv_all[1, k_at, at].T
                got = []
                for j in range(2):
                    sc = dot_nt(k_pair, q_pair * lane_masks[j]) * scale
                    sc = jnp.where(far_in <= win_ref[p * 2 + j], sc, LOW)
                    e = jnp.exp(sc - jnp.max(sc, axis=0, keepdims=True))
                    inv = 1.0 / jnp.sum(e, axis=0, keepdims=True)
                    got.append(dot(v_t, (e * inv).astype(BF16)))
                ctx[slot, :, at] = jnp.where(low_row, got[0], got[1]).T.astype(BF16)
                return carry

            lax.fori_loop(0, pairs, local_pair, 0)

        pl.when(s != donor)(functools.partial(local_block, 0))
        pl.semaphore_wait(barrier, slabs + nz - 1)

        @pl.when(s + 1 < enc)
        def _():
            remote(
                kv_ref.at[:, pl.ds(rows - HALO, HALO)],
                kv_all.at[:, pl.ds(0, HALO)],
                halo_s.at[0],
                halo_r.at[0],
                s + 1,
                g,
            ).start()

        @pl.when(s > 0)
        def _():
            remote(
                kv_ref.at[:, pl.ds(0, HALO)],
                kv_all.at[:, pl.ds(HALO + rows, HALO)],
                halo_s.at[1],
                halo_r.at[1],
                s - 1,
                g,
            ).start()

        @pl.when(is_donor)
        def _():
            local_block(0)

        load_wo(0).wait()

        @pl.when(is_donor)
        def _():
            remote(ctx.at[1], ctx.at[1], hand_s.at[1], hand_r.at[1], enc, g).start()
            remote(
                res_ref.at[pl.ds(block_at(1), sub)], slot_res.at[1], hand_s.at[0], hand_r.at[0], enc, g
            ).start()

        @pl.when(s != donor)
        def _():
            scatter_out(0, attn_part, ysend, yrecv, ys_s, yr_s)

        local_block(1)

        @pl.when(is_donor)
        def _():
            scatter_out(0, attn_part, ysend, yrecv, ys_s, yr_s)

    @pl.when(is_dec)
    def _():
        acc[0] = jnp.zeros_like(acc[0])
        pl.semaphore_wait(barrier, slabs + nz - 1)
        for b in both:
            load_cot(b).wait()
            cot_start(b)
        load_wo(0).wait()
        arrived(ctx.at[1], hand_r.at[1])

    @when_has(1)
    def _():
        scatter_out(1, attn_part, ysend, yrecv, ys_s, yr_s)

    @pl.when(is_dec)
    def _():
        load_dq().wait()
        for k in range(enc):
            remote(dq, dq, dq_s.at[k], dq_r, k, g).start()
        for b in both:
            cot_forward(b, None)

    @when_has(0)
    def _():
        scatter_own(0, attn_part)

    def start_block(b):
        total = scatter_total(b, yrecv, zrecv, yr_s, zr_s)
        hidden = (slot_res[b].astype(F32) + total).astype(BF16)
        gath[g, b] = hidden
        gather_start(b)

        @pl.when(is_enc)
        def _():
            states_ref[out_rows(b), :] = hidden

    def project(c, b):
        block = gath[c, b]
        acc[0, b] = acc[0, b] + dot(block, w_kv[0, chunk_cols(c), :])
        acc[1, b] = acc[1, b] + dot(block, w_kv[1, chunk_cols(c), :])

    def project_own(b):
        block = gath[g, b]
        acc[0, b] = dot(block, w_kv[0, chunk_cols(g), :])
        acc[1, b] = dot(block, w_kv[1, chunk_cols(g), :])

    @when_has(0)
    def _():
        scatter_join(0, yrecv, zsend, zrecv, yr_s, zs_s, zr_s)

    @when_has(1)
    def _():
        scatter_own(1, attn_part)
        scatter_join(1, yrecv, zsend, zrecv, yr_s, zs_s, zr_s)

    @when_has(0)
    def _():
        load_res(0).wait()
        start_block(0)

    @when_has(1)
    def _():
        @pl.when(is_enc)
        def _():
            load_res(1).wait()

        @pl.when(is_dec)
        def _():
            arrived(slot_res.at[1], hand_r.at[0])

        start_block(1)

        @pl.when(is_dec)
        def _():
            remote(gath.at[g, 1], back_rows, hand_s.at[0], hand_r.at[2], donor, g).start()


    @pl.when(is_dec)
    def _():
        load_wo(1).wait()

        def near(k, carry):
            back(k * 2 + y)
            return carry

        lax.fori_loop(0, nz, near, 0)
        for b in both:
            cot_finish(b, None)

        def over(k, carry):
            back(k * 2 + yo)
            return carry

        lax.fori_loop(0, nz, over, 0)
        for b in both:
            dg[b * sub : (b + 1) * sub, :] = acc[0, b].astype(BF16)
        for k in range(enc):
            remote(dg, dg, dg_s.at[k], dg_r, k, g).start()

    load_wkv().wait()

    @when_has(0)
    def _():
        project_own(0)
        gather_forward(0, project)

    @when_has(1)
    def _():
        project_own(1)
        gather_forward(1, project)

    for b in both:

        @pl.when(jnp.logical_not(has[b]))
        def _():
            stat[b, 0] = jnp.full((heads, rows), LOW, F32)
            stat[b, 1] = jnp.zeros((heads, rows), F32)
            stat[b, 2] = jnp.zeros((heads, rows), F32)
            ctx_acc[b] = jnp.zeros((cols, rows), F32)

    @pl.when(jnp.logical_not(has[0]))
    def _():
        q_acc[...] = jnp.zeros((cols, rows), F32)

    def cross_block(b):
        for i in range(2):
            kv_new[b, i] = acc[i, b].astype(BF16)
        tok_pos = key_base(b) + lax.broadcasted_iota(jnp.int32, (sub, 1), 0)
        seen = (tok_pos >= bnd_ref[0:1, enc * rows :]) & (tok_pos <= bnd_ref[1:2, enc * rows :])

        def cross_pair(p, carry):
            at = pair_cols(p)
            q_pair = dq[:, at]
            g_pair = dg[:, at]
            k_pair = kv_new[b, 0, :, at]
            v_pair = kv_new[b, 1, :, at]
            v_t = v_pair.T
            got = []
            for i in range(2):
                sc = dot_nt(k_pair, q_pair * lane_masks[i]) * scale
                sc = jnp.where(seen, sc, LOW)
                top = jnp.max(sc, axis=0, keepdims=True)
                e = jnp.exp(sc - top)
                dp = dot_nt(v_pair, g_pair * lane_masks[i])
                h = p * 2 + i
                e_buf[b, h] = e
                d_buf[b, h] = dp
                stat[b, 0, pl.ds(h, 1), :] = top
                stat[b, 1, pl.ds(h, 1), :] = jnp.sum(e, axis=0, keepdims=True)
                stat[b, 2, pl.ds(h, 1), :] = jnp.sum(e * dp, axis=0, keepdims=True)
                got.append(dot(v_t, e.astype(BF16)))
            ctx_acc[b, pair_cols(p), :] = jnp.where(low_row, got[0], got[1])
            return carry

        lax.fori_loop(0, pairs, cross_pair, 0)

    @when_has(0)
    def _():
        gather_finish(0, project)
        arrived(dq, dq_r)
        arrived(dg, dg_r)
        cross_block(0)

    @when_has(1)
    def _():
        gather_finish(1, project)
        cross_block(1)

    own_top = jnp.maximum(stat[0, 0], stat[1, 0])
    lift = [jnp.exp(stat[b, 0] - own_top) for b in both]
    stat_all[s, 0] = own_top
    stat_all[s, 1] = lift[0] * stat[0, 1] + lift[1] * stat[1, 1]
    stat_all[s, 2] = lift[0] * stat[0, 2] + lift[1] * stat[1, 2]
    for k in range(1, slabs):
        to = lax.rem(s + k, slabs)
        remote(stat_all.at[s], stat_all.at[s], st_s.at[k - 1], st_r.at[s], to, g).start()
    for h in range(heads):
        at = slice(h * HD, (h + 1) * HD)
        tbuf[at, :] = (
            lift[0][h : h + 1, :] * ctx_acc[0, at, :] + lift[1][h : h + 1, :] * ctx_acc[1, at, :]
        ).astype(BF16)

    @pl.when(is_enc)
    def _():
        remote(tbuf, ctx_in.at[s], cx_s, cx_r.at[s], enc, g).start()

    for k in range(1, slabs):
        at = lax.rem(s + k, slabs)
        arrived(stat_all.at[at], st_r.at[at])
    top = stat_all[0, 0]
    for i in range(1, slabs):
        top = jnp.maximum(top, stat_all[i, 0])
    shifts = [jnp.exp(stat_all[i, 0] - top) for i in range(slabs)]
    total = shifts[0] * stat_all[0, 1]
    dots = shifts[0] * stat_all[0, 2]
    for i in range(1, slabs):
        total = total + shifts[i] * stat_all[i, 1]
        dots = dots + shifts[i] * stat_all[i, 2]
    inv_total = 1.0 / total
    for b in both:
        fac[b] = jnp.exp(stat[b, 0] - top) * inv_total
    fac[SLOTS] = dots * inv_total

    def grad_block(b):
        def grad_pair(p, carry):
            at = pair_cols(p)
            q_pair = dq[:, at]
            g_pair = dg[:, at]
            k_t = kv_new[b, 0, :, at].T
            kg, vg, qg = [], [], []
            for i in range(2):
                h = p * 2 + i
                w = e_buf[b, h] * fac[b, pl.ds(h, 1), :]
                ds = (w * (d_buf[b, h] - fac[SLOTS, pl.ds(h, 1), :])).astype(BF16)
                vg.append(dot(w.astype(BF16), g_pair))
                kg.append(dot(ds, q_pair))
                qg.append(dot(k_t, ds))
            kvg[b, 0, :, at] = (scale * jnp.where(low_lane, kg[0], kg[1])).astype(BF16)
            kvg[b, 1, :, at] = jnp.where(low_lane, vg[0], vg[1]).astype(BF16)
            mine = scale * jnp.where(low_row, qg[0], qg[1])
            q_acc[pair_cols(p), :] = mine if b == 0 else q_acc[pair_cols(p), :] + mine
            return carry

        lax.fori_loop(0, pairs, grad_pair, 0)

    def grad_part(b, c):
        return (
            dot_nt(kvg[b, 0], w_kv[0, chunk_cols(c), :]) + dot_nt(kvg[b, 1], w_kv[1, chunk_cols(c), :])
        ).astype(BF16)

    def final_out(b, part):
        scatter_out(b, part, ysend2, yrecv2, ys2_s, yr2_s)

    @when_has(0)
    def _():
        grad_block(0)
        final_out(0, grad_part)
        scatter_own(0, grad_part)

    @when_has(1)
    def _():
        grad_block(1)

    @pl.when(is_enc)
    def _():
        qg_buf[...] = q_acc[...].astype(BF16)

        @pl.when(is_donor)
        def _():
            arrived(kvg.at[1], hand_r.at[3])

        final_out(1, grad_part)
        remote(qg_buf, qg_in.at[s], qg_s, qg_r.at[s], enc, g).start()
        load_base(cot_ref).wait()
        scatter_join(0, yrecv2, zsend2, zrecv2, yr2_s, zs2_s, zr2_s)
        scatter_own(1, grad_part)
        scatter_join(1, yrecv2, zsend2, zrecv2, yr2_s, zs2_s, zr2_s)
        for b in both:
            final_in(b, grads_ref)

        @pl.when(is_donor)
        def _():
            arrived(back_rows, hand_r.at[2])
            states_ref[out_rows(1), :] = back_rows[...]
            arrived(slot_res.at[1], hand_s.at[0])
            arrived(ctx.at[1], hand_s.at[1])
            load_res(1).wait()

        @pl.when(s + 1 < enc)
        def _():
            arrived(kv_ref.at[:, pl.ds(rows - HALO, HALO)], halo_s.at[0])

        @pl.when(s > 0)
        def _():
            arrived(kv_ref.at[:, pl.ds(0, HALO)], halo_s.at[1])

        arrived(tbuf, cx_s)
        arrived(qg_buf, qg_s)

    @pl.when(is_dec)
    def _():
        remote(kvg.at[1], kvg.at[1], hand_s.at[1], hand_r.at[3], donor, g).start()
        ctx_in[enc] = tbuf[...]
        for k in range(enc):
            arrived(ctx_in.at[k], cx_r.at[k])
        shares = [shifts[k] * inv_total for k in range(slabs)]
        for p in range(pairs):
            mixed = []
            for h in (2 * p, 2 * p + 1):
                at = slice(h * HD, (h + 1) * HD)
                part = shares[0][h : h + 1, :] * ctx_in[0, at, :].astype(F32)
                for k in range(1, slabs):
                    part = part + shares[k][h : h + 1, :] * ctx_in[k, at, :].astype(F32)
                mixed.append(part)
            dctx[:, p * PAIR : (p + 1) * PAIR] = jnp.concatenate(mixed, axis=0).T.astype(BF16)

        def dec_part(b, c):
            return dot(dctx[b * sub : (b + 1) * sub, :], w_out[1, :, chunk_cols(c)]).astype(BF16)

        for b in both:
            final_out(b, dec_part)
        load_base(res_ref).wait()
        for b in both:
            scatter_own(b, dec_part)
            scatter_join(b, yrecv2, zsend2, zrecv2, yr2_s, zs2_s, zr2_s)
        for k in range(enc):
            arrived(qg_in.at[k], qg_r.at[k])
        for p in range(pairs):
            at = slice(p * PAIR, (p + 1) * PAIR)
            part = q_acc[at, :]
            for k in range(enc):
                part = part + qg_in[k, at, :].astype(F32)
            grads_ref[:, at] = part.T.astype(BF16)
        for b in both:
            final_in(b, states_ref)
        for k in range(enc):
            arrived(dq, dq_s.at[k])
            arrived(dg, dg_s.at[k])
        for b in both:
            cot_end(b)
        arrived(gath.at[g, 1], hand_s.at[0])
        arrived(kvg.at[1], hand_s.at[1])

    for b in both:

        @when_has(b)
        def _():
            end_scatter(b, ysend, zsend, ys_s, zs_s)
            gather_end(b)

        end_scatter(b, ysend2, zsend2, ys2_s, zs2_s)
    for k in range(1, slabs):
        arrived(stat_all.at[s], st_s.at[k - 1])


def deliver(states_in, grads_in, states_out, grads_out):
    states_out[...] = states_in[...]
    grads_out[...] = grads_in[...]


def layer(slabs, groups, queries, keys_values, residual, cotangent, out_weight, kv_weight, bounds, windows):
    rows, cols = queries.shape
    heads = cols // HD
    nz = groups // 2
    enc = slabs - 1
    sub = rows // SLOTS
    width = out_weight.shape[2]
    dma = pltpu.SemaphoreType.DMA
    parts = lambda: pltpu.VMEM((SLOTS, nz, sub, cols), BF16)
    vmem = pl.BlockSpec(memory_space=pltpu.VMEM)
    hbm = pl.BlockSpec(memory_space=pl.ANY)
    states, grads = pl.pallas_call(
        functools.partial(layer_kernel, slabs, groups),
        out_shape=(jax.ShapeDtypeStruct((rows, cols), BF16),) * 2,
        in_specs=[hbm] * 6 + [vmem, pl.BlockSpec(memory_space=pltpu.SMEM)],
        out_specs=(vmem, vmem),
        scratch_shapes=[
            pltpu.VMEM((2, cols, width), BF16),
            pltpu.VMEM((2, width, cols), BF16),
            pltpu.VMEM((2, rows + 2 * HALO, cols), BF16),
            pltpu.VMEM((rows, cols), BF16),
            pltpu.VMEM((rows, cols), BF16),
            pltpu.VMEM((SLOTS, sub, cols), BF16),
            pltpu.VMEM((SLOTS, sub, cols), BF16),
        ]
        + [parts() for _ in range(9)]
        + [
            pltpu.VMEM((groups, SLOTS, sub, cols), BF16),
            pltpu.VMEM((groups, SLOTS, sub, cols), BF16),
            pltpu.VMEM((2, SLOTS, sub, cols), F32),
            pltpu.VMEM((SLOTS, 2, sub, cols), BF16),
            pltpu.VMEM((rows, cols), BF16),
            pltpu.VMEM((rows, cols), BF16),
            pltpu.VMEM((SLOTS, heads, sub, rows), F32),
            pltpu.VMEM((SLOTS, heads, sub, rows), F32),
            pltpu.VMEM((SLOTS, 3, heads, rows), F32),
            pltpu.VMEM((SLOTS, cols, rows), F32),
            pltpu.VMEM((slabs, 3, heads, rows), F32),
            pltpu.VMEM((SLOTS + 1, heads, rows), F32),
            pltpu.VMEM((cols, rows), BF16),
            pltpu.VMEM((slabs, cols, rows), BF16),
            pltpu.VMEM((cols, rows), F32),
            pltpu.VMEM((cols, rows), BF16),
            pltpu.VMEM((enc, cols, rows), BF16),
            pltpu.VMEM((SLOTS, 2, sub, cols), BF16),
            pltpu.VMEM((rows, cols), BF16),
            pltpu.VMEM((sub, cols), BF16),
            dma((3,)),
            dma((5,)),
            dma((2,)),
            dma((2,)),
        ]
        + [dma((SLOTS, nz))] * 8
        + [dma((nz, SLOTS))] * 8
        + [
            dma((enc,)),
            dma,
            dma((enc,)),
            dma,
            dma((enc,)),
            dma((slabs,)),
            dma,
            dma((enc,)),
            dma,
            dma((enc,)),
            dma((2,)),
            dma((4,)),
        ],
        compiler_params=pltpu.CompilerParams(
            collective_id=0, has_side_effects=True, vmem_limit_bytes=60 * 1024 * 1024
        ),
    )(queries, keys_values, residual, cotangent, out_weight, kv_weight, bounds, windows)
    return pl.pallas_call(
        deliver,
        out_shape=(jax.ShapeDtypeStruct((rows, cols), BF16),) * 2,
        in_specs=[vmem] * 2,
        out_specs=(vmem, vmem),
    )(states, grads)


def one_decoder_slab(mesh):
    slabs, groups = mesh.shape["seq"], mesh.shape["mp"]
    return slabs == 4 and groups == 8


def solution(mesh):
    body = shards
    if one_decoder_slab(mesh):
        body = functools.partial(layer, mesh.shape["seq"], mesh.shape["mp"])

    return jax.shard_map(
        body,
        mesh=mesh,
        in_specs=(
            P("seq", "mp"),
            P(None, "seq", "mp"),
            P("seq", "mp"),
            P("seq", "mp"),
            P(None, "mp", None),
            P(None, None, "mp"),
            P(),
            P("mp"),
        ),
        out_specs=(P("seq", "mp"), P("seq", "mp")),
        check_vma=False,
    )
```
